512 devices in a mesh: tm: 128 (over y, z, core), head: 4 (over x).
Axes of the slice: x: 4, y: 4, z: 16, core: 2. Of those that a mesh axis runs over, the one named last changes fastest.
Arguments:
- tokens: bfloat16 [32768, 1024], P('tm'), may hold values from -24 to 24
- q_weight: bfloat16 [1024, 1024], P(None, 'head'), may hold values from -2 to 2
- k_weight: bfloat16 [1024, 1024], P(None, 'head'), may hold values from -2 to 2
- v_weight: bfloat16 [1024, 1024], P(None, 'head'), may hold values from -0.1875 to 0.1875
- o_weight: bfloat16 [1024, 1024], P('head'), may hold values from -0.1875 to 0.1875
- rand_blocks: int32 [256, 3], P('tm'), may hold values from 0 to 255, as said below
- global_pos: int32 [256], replicated, may hold values from 0 to 32767, as said below
Outputs:
- mixed_out: bfloat16 [32768, 1024], P(('tm', 'head'))
The draws below stay inside these ranges and needn't reach their ends.
Inputs may be any that keep to these rules, and one draw needn't show every extreme that they name: rand_blocks[b, r] names a block whose shard index (block // 2) differs from that of b by at most 2; in every draw some entry differs by exactly 2. `global_pos`: 256 distinct positions in ascending order.
All inputs are finite; a program needn't handle non-finite values.
Results may differ from the reference program's by a relative error of at most 0.011.
Values may be sent and summed in bfloat16 or wider, within the bound.
A program may use at most 64 MiB of HBM per device.

```python
import math
import jax
import jax.numpy as jnp
from jax import lax

D = 1024
HEADS = 16
HEAD_DIM = 64
BLOCK = 128
GLOBALS = 256
RAND = 3
SPREAD = 2
TOK_DEV = 256
TOKENS = 32768
BLOCKS = 256


def weight_matrix(key):
    return jnp.clip(jax.random.normal(key, (D, D), jnp.float32), -6.0, 6.0) * math.sqrt(3.0 / D)


def draw_q_weight(key, part):
    return weight_matrix(jax.random.fold_in(key, 11)).astype(jnp.bfloat16)


def draw_k_weight(key, part):
    own_matrix = weight_matrix(jax.random.fold_in(key, 12))
    return own_matrix.astype(jnp.bfloat16)


def draw_tokens(key, part):
    drawn_rows = jnp.clip(jax.random.normal(key, (TOKENS, D), jnp.float32), -6.0, 6.0)
    return drawn_rows.astype(jnp.bfloat16)


def draw_rand_blocks(key, part):
    per_shard = TOK_DEV // BLOCK
    shard_total = BLOCKS // per_shard
    home_shard = jnp.arange(BLOCKS, dtype=jnp.int32)[:, None] // per_shard
    lowest = jnp.maximum(home_shard - SPREAD, 0)
    highest = jnp.minimum(home_shard + SPREAD, shard_total - 1)
    first_key, second_key = jax.random.split(key)
    picked_shard = lowest + jax.random.randint(first_key, (BLOCKS, RAND), 0, highest - lowest + 1)
    picked_shard = picked_shard.at[0, 0].set(SPREAD)
    inner_block = jax.random.randint(second_key, (BLOCKS, RAND), 0, per_shard)
    return (picked_shard * per_shard + inner_block).astype(jnp.int32)


def draw_global_pos(key, part):
    shuffled = jax.random.permutation(key, jnp.arange(TOKENS, dtype=jnp.int32))
    return jnp.sort(shuffled[:GLOBALS]).astype(jnp.int32)


def steps_of(stream_key, dims, pieces, least, high):
    factor_of = 1.0
    for axis_at, shards_of in pieces:
        steps = jax.random.uniform(jax.random.fold_in(jax.random.fold_in(stream_key, 6), axis_at), (shards_of,), jnp.float32, least / len(pieces), high / len(pieces))
        factor_of = factor_of * jnp.repeat(jnp.exp(steps), dims[axis_at] // shards_of).reshape((-1,) + (1,) * (len(dims) - 1 - axis_at))
    return factor_of


def centred(own_key, extent, scale, most, pieces=(), held_as=jnp.bfloat16):
    values = scale * jax.random.normal(own_key, extent, jnp.float32)
    if pieces:
        values = values * steps_of(own_key, extent, pieces, -0.22, 0.18)
    return jnp.clip(values, -most, most).astype(held_as)


def setup_inputs(seed: int = 0) -> dict:
    key_of = jax.random.split(jax.random.key(seed), 8)
    tokens = draw_tokens(jax.random.fold_in(key_of[7], 71), 0)
    q_weight = draw_q_weight(jax.random.fold_in(key_of[7], 71), 0)
    k_weight = draw_k_weight(jax.random.fold_in(key_of[7], 71), 0)
    v_weight = centred(key_of[3], (D, D), D ** -0.5, 0.1875, ((1, 4),))
    o_weight = centred(key_of[4], (D, D), D ** -0.5, 0.1875, ((0, 4),))
    rand_blocks = draw_rand_blocks(jax.random.fold_in(key_of[7], 71), 0)
    global_pos = draw_global_pos(jax.random.fold_in(key_of[7], 71), 0)
    return dict(tokens=tokens, q_weight=q_weight, k_weight=k_weight, v_weight=v_weight, o_weight=o_weight, rand_blocks=rand_blocks, global_pos=global_pos)


def reference(tokens, q_weight, k_weight, v_weight, o_weight, rand_blocks, global_pos):
    score_scale = HEAD_DIM ** -0.5
    queries = jnp.dot(tokens, q_weight, preferred_element_type=jnp.float32).astype(jnp.bfloat16).reshape(TOKENS, HEADS, HEAD_DIM)
    keys_all = jnp.dot(tokens, k_weight, preferred_element_type=jnp.float32).astype(jnp.bfloat16).reshape(TOKENS, HEADS, HEAD_DIM)
    values_all = jnp.dot(tokens, v_weight, preferred_element_type=jnp.float32).astype(jnp.bfloat16).reshape(TOKENS, HEADS, HEAD_DIM)
    glob_q = queries[global_pos]
    glob_k = keys_all[global_pos]
    glob_v = values_all[global_pos]

    def global_head(operands):
        query_head, key_head, value_head = operands
        scores = jnp.dot(query_head, key_head.T, preferred_element_type=jnp.float32) * score_scale
        weights = jnp.exp(scores - jnp.max(scores, axis=1, keepdims=True))
        summed = jnp.dot(weights, value_head.astype(jnp.float32), precision=lax.Precision.HIGHEST)
        return (summed / jnp.sum(weights, axis=1, keepdims=True)).astype(jnp.bfloat16)

    global_out = lax.map(global_head, (jnp.transpose(glob_q, (1, 0, 2)), jnp.transpose(keys_all, (1, 0, 2)), jnp.transpose(values_all, (1, 0, 2))))
    key_blocks = keys_all.reshape(BLOCKS, BLOCK, HEADS, HEAD_DIM)
    value_blocks = values_all.reshape(BLOCKS, BLOCK, HEADS, HEAD_DIM)
    padded_k = jnp.pad(keys_all, ((2 * BLOCK, BLOCK), (0, 0), (0, 0)))
    padded_v = jnp.pad(values_all, ((2 * BLOCK, BLOCK), (0, 0), (0, 0)))

    def one_block(block_id):
        first_row = (block_id * BLOCK).astype(jnp.int32)
        query_block = lax.dynamic_slice_in_dim(queries, first_row, BLOCK, 0)
        window_k = lax.dynamic_slice_in_dim(padded_k, first_row, 4 * BLOCK, 0)
        window_v = lax.dynamic_slice_in_dim(padded_v, first_row, 4 * BLOCK, 0)
        random_k = key_blocks[rand_blocks[block_id]].reshape(RAND * BLOCK, HEADS, HEAD_DIM)
        random_v = value_blocks[rand_blocks[block_id]].reshape(RAND * BLOCK, HEADS, HEAD_DIM)
        keys_block = jnp.concatenate([window_k, random_k, glob_k], axis=0)
        values_block = jnp.concatenate([window_v, random_v, glob_v], axis=0)
        spots = first_row - 2 * BLOCK + jnp.arange(4 * BLOCK, dtype=jnp.int32)
        valid = jnp.concatenate([(spots >= 0) & (spots < TOKENS), jnp.ones((RAND * BLOCK + GLOBALS,), dtype=bool)])
        scores = jnp.einsum("qhd,khd->hqk", query_block.astype(jnp.float32), keys_block.astype(jnp.float32)) * score_scale
        scores = jnp.where(valid[None, None, :], scores, -jnp.inf)
        peak = jnp.max(scores, axis=2, keepdims=True)
        expo = jnp.exp(scores - peak)
        denominator = jnp.sum(expo, axis=2)
        rounded = lax.optimization_barrier(expo.astype(jnp.bfloat16)).astype(jnp.float32)
        numerator = jnp.einsum("hqk,khd->qhd", rounded, values_block.astype(jnp.float32))
        return (numerator / jnp.transpose(denominator)[:, :, None]).astype(jnp.bfloat16)

    blocks_out = lax.map(one_block, jnp.arange(BLOCKS, dtype=jnp.int32))
    attended = blocks_out.reshape(TOKENS, D)
    attended = attended.at[global_pos].set(jnp.transpose(global_out, (1, 0, 2)).reshape(GLOBALS, D))
    return jnp.dot(attended, o_weight, preferred_element_type=jnp.float32).astype(jnp.bfloat16)
```

```python
import functools
import math

import jax
import jax.numpy as jnp
from jax import lax
from jax.experimental import pallas as pl
from jax.experimental.pallas import tpu as pltpu
from jax.sharding import PartitionSpec as P

HEAD_DIM = 64
BLOCK = 128
GLOBALS = 256
RAND = 3
SPREAD = 2
TOK = 256
FEATS = 256
HEADS_HERE = FEATS // HEAD_DIM
LOG2_SCALE = math.log2(math.e) / math.sqrt(HEAD_DIM)
NEG = -1e30
MESH = pl.DeviceIdType.MESH
F32 = jnp.float32
BF16 = jnp.bfloat16


def dot_nn(a, b):
    return jnp.dot(a, b, preferred_element_type=F32)


def dot_nt(a, b):
    return lax.dot_general(a, b, (((1,), (1,)), ((), ())), preferred_element_type=F32)


def split_of(shards):
    return {128: (4, 4, 4), 16: (2, 2, 2), 64: (4, 2, 4)}[shards]


def scratch_of(split, heads, d):
    y_n, zn_n, zf_n = split
    r = 2 * y_n
    ch = GLOBALS // r
    vm = pltpu.VMEM

    def stream(tag, width):
        return {
            tag + "part": vm((GLOBALS, width), BF16),
            tag + "a": vm((r - 1, ch, width), BF16),
            tag + "bs": vm((ch, width), BF16),
            tag + "b": vm((zn_n - 1, ch, width), BF16),
            tag + "cs": vm((ch, width), BF16),
            tag + "c": vm((zf_n - 1, ch, width), BF16),
            tag + "full": vm((GLOBALS, width), BF16),
        }

    out = {
        "tok": vm((TOK, d), BF16),
        "wq": vm((d, FEATS), BF16),
        "wk": vm((d, FEATS), BF16),
        "wv": vm((d, FEATS), BF16),
        "osl": vm((heads, FEATS, d), BF16),
        "asl": vm((heads - 1, TOK // heads, FEATS), BF16),
        "att": vm((TOK, FEATS), BF16),
        "attl": vm((TOK, FEATS), F32),
        "att_t": vm((FEATS, TOK), F32),
        "q": vm((TOK, FEATS), BF16),
        "kx": vm((10, BLOCK, FEATS), BF16),
        "vx": vm((10, FEATS, BLOCK), BF16),
        "gvt": vm((2, FEATS, BLOCK), BF16),
        "s": vm((9, BLOCK, 2 * BLOCK), F32),
        "pick": vm((TOK, GLOBALS), BF16),
        "lpart": vm((HEADS_HERE, 1, GLOBALS), F32),
        "la": vm((r - 1, 1, GLOBALS), F32),
        "lbs": vm((1, 1, GLOBALS), F32),
        "lb": vm((zn_n - 1, 1, GLOBALS), F32),
        "lcs": vm((1, 1, GLOBALS), F32),
        "lc": vm((zf_n - 1, 1, GLOBALS), F32),
    }
    out.update(stream("q_", FEATS))
    out.update(stream("kv_", 2 * FEATS))
    out.update(stream("o_", GLOBALS))
    copies = 3 * (2 * (r - 1) + zn_n + zf_n - 2) + (r - 1 + zn_n + zf_n - 2) + 8 + 2 * (heads - 1)
    out["send"] = pltpu.SemaphoreType.DMA((copies,))
    out["recv"] = pltpu.SemaphoreType.DMA((copies,))
    out["load"] = pltpu.SemaphoreType.DMA((5,))
    return out


def kernel(split, heads, names, tok_h, wq_h, wk_h, wv_h, ow_h, rand_s, grow_v, out_v, *scratch):
    m = dict(zip(names, scratch))
    y_n, zn_n, zf_n = split
    r = 2 * y_n
    ch = GLOBALS // r
    shards = r * zn_n * zf_n
    tm = lax.axis_index("tm")
    hd = lax.axis_index("head")
    z_n = zn_n * zf_n
    y = tm // (2 * z_n)
    z = (tm // 2) % z_n
    c = tm % 2
    j = y * 2 + c
    zn = z % zn_n
    zf = z // zn_n

    def dev_j(jj):
        return ((jj // 2) * (2 * z_n) + z * 2 + jj % 2, hd)

    def dev_z(zz):
        return (y * (2 * z_n) + zz * 2 + c, hd)

    group_j = [dev_j((j + d) % r) for d in range(1, r)]
    group_n = [dev_z(zf * zn_n + (zn + d) % zn_n) for d in range(1, zn_n)]
    group_f = [dev_z(((zf + d) % zf_n) * zn_n + zn) for d in range(1, zf_n)]
    group_h = [(tm, (hd + d) % heads) for d in range(1, heads)]
    steps_w = (1, -1, 2, -2)
    group_w = [((tm + d + shards) % shards, hd) for d in steps_w]
    everyone = group_j + group_n + group_f + group_h + group_w

    loads = [
        pltpu.make_async_copy(src, m[dst], m["load"].at[i])
        for i, (src, dst) in enumerate(
            ((tok_h, "tok"), (wq_h, "wq"), (wk_h, "wk"), (wv_h, "wv"))
        )
    ]
    loads.append(pltpu.make_async_copy(ow_h, m["osl"].at[0], m["load"].at[4]))
    for copy in loads:
        copy.start()

    barrier = pltpu.get_barrier_semaphore()
    for dev in everyone:
        pl.semaphore_signal(barrier, inc=1, device_id=dev, device_id_type=MESH)

    count = [0]
    started = []

    def send(src, dst, dev):
        n = count[0]
        count[0] += 1
        copy = pltpu.make_async_remote_copy(
            src_ref=src,
            dst_ref=dst,
            send_sem=m["send"].at[n],
            recv_sem=m["recv"].at[n],
            device_id=dev,
            device_id_type=MESH,
        )
        copy.start()
        started.append(copy)
        return copy

    def rows(jj):
        return pl.ds(pl.multiple_of(jj * ch, ch), ch)

    def start_a(tag):
        part = m[tag + "part"]
        return [
            send(part.at[rows((j + d) % r)], m[tag + "a"].at[d - 1], group_j[d - 1])
            for d in range(1, r)
        ]

    def gather(first, copies, slots):
        total = first.astype(F32)
        for n, copy in enumerate(copies):
            copy.wait_recv()
            total = total + slots[n].astype(F32)
        return total.astype(BF16)

    def start_b(tag):
        return [send(m[tag + "bs"], m[tag + "b"].at[d], group_n[d]) for d in range(zn_n - 1)]

    def start_c(tag):
        return [send(m[tag + "cs"], m[tag + "c"].at[d], group_f[d]) for d in range(zf_n - 1)]

    def start_d(tag):
        mine = m[tag + "full"].at[rows(j)]
        return [send(mine, mine, group_j[d]) for d in range(r - 1)]

    loads[0].wait()
    loads[1].wait()
    q = dot_nn(m["tok"][...], m["wq"][...]).astype(BF16)
    m["q"][...] = q
    spots = lax.broadcasted_iota(jnp.int32, (TOK, GLOBALS), 0) + tm * TOK
    pick = jnp.where(spots == grow_v[...], 1.0, 0.0).astype(F32)
    m["pick"][...] = pick.astype(BF16)
    pick_t = pick.T.astype(BF16)
    m["q_part"][...] = dot_nn(pick_t, q).astype(BF16)
    pl.semaphore_wait(barrier, len(everyone))
    qa = start_a("q_")

    loads[4].wait()
    ow = [send(m["osl"].at[0], m["osl"].at[d + 1], group_h[d]) for d in range(heads - 1)]

    loads[2].wait()
    k = dot_nn(m["tok"][...], m["wk"][...]).astype(BF16)
    m["kv_part"][:, :FEATS] = dot_nn(pick_t, k).astype(BF16)
    for b in range(2):
        m["kx"][4 + b] = k[b * BLOCK : (b + 1) * BLOCK]
    loads[3].wait()
    v32 = dot_nn(m["tok"][...], m["wv"][...])
    m["kv_part"][:, FEATS:] = dot_nn(pick_t, v32.astype(BF16)).astype(BF16)
    kva = start_a("kv_")
    v_t = v32.T.astype(BF16)
    for b in range(2):
        m["vx"][4 + b] = v_t[:, b * BLOCK : (b + 1) * BLOCK]

    m["q_bs"][...] = gather(m["q_part"][rows(j)], qa, m["q_a"])
    qb = start_b("q_")
    m["kv_bs"][...] = gather(m["kv_part"][rows(j)], kva, m["kv_a"])
    kvb = start_b("kv_")
    m["q_cs"][...] = gather(m["q_bs"][...], qb, m["q_b"])
    qc = start_c("q_")
    m["kv_cs"][...] = gather(m["kv_bs"][...], kvb, m["kv_b"])
    kvc = start_c("kv_")

    window = []
    for step, dev in zip(steps_w, group_w):
        slot = 2 * (SPREAD - step)
        for name in ("kx", "vx"):
            window.append(send(m[name].at[pl.ds(4, 2)], m[name].at[pl.ds(slot, 2)], dev))

    m["q_full"][rows(j)] = gather(m["q_cs"][...], qc, m["q_c"])
    qd = start_d("q_")

    lane_head = lax.broadcasted_iota(jnp.int32, (1, FEATS), 1) // HEAD_DIM

    def head_mask(h):
        return jnp.where(lane_head == h, 1.0, 0.0).astype(BF16)

    for copy in qd:
        copy.wait_recv()
    gq = m["q_full"][...]
    for h in range(HEADS_HERE):
        gq_h = gq * head_mask(h)
        s0 = dot_nt(m["kx"][4], gq_h) * LOG2_SCALE
        s1 = dot_nt(m["kx"][5], gq_h) * LOG2_SCALE
        peak = jnp.maximum(jnp.max(s0, axis=0, keepdims=True), jnp.max(s1, axis=0, keepdims=True))
        p0 = jnp.exp2(s0 - peak)
        p1 = jnp.exp2(s1 - peak)
        total = jnp.sum(p0, axis=0, keepdims=True) + jnp.sum(p1, axis=0, keepdims=True)
        feats = pl.ds(h * HEAD_DIM, HEAD_DIM)
        acc = dot_nn(m["vx"][4, feats, :], p0.astype(BF16))
        acc = acc + dot_nn(m["vx"][5, feats, :], p1.astype(BF16))
        m["o_part"][feats, :] = (acc / total).astype(BF16)
        m["lpart"][h] = peak + jnp.log2(total)

    def head_of(jj):
        return (jj * HEADS_HERE) // r

    oa = start_a("o_")
    la = [
        send(m["lpart"].at[head_of((j + d) % r)], m["la"].at[d - 1], group_j[d - 1])
        for d in range(1, r)
    ]

    def combine(o_first, l_first, o_copies, l_copies, o_slots, l_slots):
        for copy in o_copies + l_copies:
            copy.wait_recv()
        size = len(o_copies)
        logs = [l_first] + [l_slots[n] for n in range(size)]
        peak = functools.reduce(jnp.maximum, logs)
        shares = [jnp.exp2(x - peak) for x in logs]
        total = functools.reduce(jnp.add, shares)
        acc = o_first.astype(F32) * shares[0]
        for n in range(size):
            acc = acc + o_slots[n].astype(F32) * shares[n + 1]
        return (acc / total).astype(BF16), peak + jnp.log2(total)

    o, l = combine(m["o_part"][rows(j)], m["lpart"][head_of(j)], oa, la, m["o_a"], m["la"])
    m["o_bs"][...] = o
    m["lbs"][0] = l
    ob = start_b("o_")
    lb = [send(m["lbs"].at[0], m["lb"].at[d], group_n[d]) for d in range(zn_n - 1)]

    m["kv_full"][rows(j)] = gather(m["kv_cs"][...], kvc, m["kv_c"])
    kvd = start_d("kv_")

    o, l = combine(m["o_bs"][...], m["lbs"][0], ob, lb, m["o_b"], m["lb"])
    m["o_cs"][...] = o
    m["lcs"][0] = l
    oc = start_c("o_")
    lc = [send(m["lcs"].at[0], m["lc"].at[d], group_f[d]) for d in range(zf_n - 1)]

    for copy in kvd + window:
        copy.wait_recv()
    gv_t = m["kv_full"][:, FEATS:].astype(F32).T.astype(BF16)
    for b in range(2):
        m["gvt"][b] = gv_t[:, b * BLOCK : (b + 1) * BLOCK]
    blocks = 2 * shards

    def attend(step, carry):
        jb = step // 2
        pair = step % 2
        qb_here = m["q"][pl.ds(pl.multiple_of(jb * BLOCK, BLOCK), BLOCK), :]
        q2 = jnp.concatenate(
            [qb_here * head_mask(2 * pair), qb_here * head_mask(2 * pair + 1)], axis=0
        )
        feats = pl.ds(pl.multiple_of(pair * 2 * HEAD_DIM, 2 * HEAD_DIM), 2 * HEAD_DIM)
        spots_x = [2 + jb + w for w in range(4)]
        spots_x += [jnp.clip(rand_s[jb, n] - 2 * tm + 2 * SPREAD, 0, 9) for n in range(RAND)]
        peak = None
        for n in range(9):
            if n < 7:
                keys = m["kx"][spots_x[n]]
            else:
                keys = m["kv_full"][pl.ds((n - 7) * BLOCK, BLOCK), :FEATS]
            s = dot_nt(keys, q2) * LOG2_SCALE
            if n in (0, 1, 3):
                block = 2 * tm + jb + n - 2
                inside = (block >= 0) & (block < blocks)
                s = jnp.where(inside, s, NEG)
            m["s"][n] = s
            top = jnp.max(s, axis=0, keepdims=True)
            peak = top if peak is None else jnp.maximum(peak, top)
        total = jnp.zeros((1, 2 * BLOCK), F32)
        acc = jnp.zeros((2 * HEAD_DIM, 2 * BLOCK), F32)
        for n in range(9):
            e = jnp.exp2(m["s"][n] - peak)
            total = total + jnp.sum(e, axis=0, keepdims=True)
            if n < 7:
                values = m["vx"][spots_x[n], feats, :]
            else:
                values = m["gvt"][n - 7, feats, :]
            acc = acc + dot_nn(values, e.astype(BF16))
        acc = acc / total
        lanes = pl.ds(pl.multiple_of(jb * BLOCK, BLOCK), BLOCK)
        for n in range(2):
            here = pl.ds(pl.multiple_of(pair * 2 * HEAD_DIM + n * HEAD_DIM, HEAD_DIM), HEAD_DIM)
            m["att_t"][here, lanes] = acc[
                n * HEAD_DIM : (n + 1) * HEAD_DIM, n * BLOCK : (n + 1) * BLOCK
            ]
        return carry

    lax.fori_loop(0, 4, attend, 0)
    is_global = jnp.max(m["pick"][...].astype(F32), axis=1, keepdims=True)
    m["attl"][...] = jnp.where(is_global > 0.5, 0.0, m["att_t"][...].T)

    o, l = combine(m["o_cs"][...], m["lcs"][0], oc, lc, m["o_c"], m["lc"])
    m["o_full"][rows(j)] = o
    od = start_d("o_")
    for copy in od:
        copy.wait_recv()

    placed = dot_nt(m["pick"][...], m["o_full"][...])
    m["att"][...] = (placed + m["attl"][...]).astype(BF16)
    per = TOK // heads

    def out_rows(hh):
        return pl.ds(pl.multiple_of(hh * per, per), per)

    ax = [
        send(m["att"].at[out_rows((hd + d + 1) % heads)], m["asl"].at[d], group_h[d])
        for d in range(heads - 1)
    ]
    mixed = dot_nn(m["att"][out_rows(hd)], m["osl"][0])
    for d in range(heads - 1):
        ow[d].wait_recv()
        ax[d].wait_recv()
        mixed = mixed + dot_nn(m["asl"][d], m["osl"][d + 1])
    out_v[...] = mixed.astype(BF16)
    for copy in started:
        copy.wait_send()


def shards_fn(tokens, q_weight, k_weight, v_weight, o_weight, rand_blocks, global_pos):
    shards = lax.axis_size("tm")
    heads = lax.axis_size("head")
    split = split_of(shards)
    d = tokens.shape[1]
    scratch = scratch_of(split, heads, d)
    hbm = pl.BlockSpec(memory_space=pl.ANY)
    return pl.pallas_call(
        functools.partial(kernel, split, heads, list(scratch)),
        out_shape=jax.ShapeDtypeStruct((TOK // heads, d), BF16),
        in_specs=[hbm] * 5
        + [
            pl.BlockSpec(memory_space=pltpu.SMEM),
            pl.BlockSpec(memory_space=pltpu.VMEM),
        ],
        out_specs=pl.BlockSpec(memory_space=pltpu.VMEM),
        scratch_shapes=list(scratch.values()),
        compiler_params=pltpu.CompilerParams(
            collective_id=0, has_side_effects=True, vmem_limit_bytes=48 << 20
        ),
        name="layer",
    )(
        tokens,
        q_weight,
        k_weight,
        v_weight,
        o_weight,
        rand_blocks,
        global_pos.reshape(1, GLOBALS),
    )


def solution(mesh):
    placed = (
        P("tm", None),
        P(None, "head"),
        P(None, "head"),
        P(None, "head"),
        P("head", None),
        P("tm", None),
        P(),
    )
    return jax.shard_map(
        shards_fn, mesh=mesh, in_specs=placed, out_specs=P(("tm", "head"), None), check_vma=False
    )
```

```python
import functools
import math

import jax
import jax.numpy as jnp
from jax import lax
from jax.experimental import pallas as pl
from jax.experimental.pallas import tpu as pltpu
from jax.sharding import PartitionSpec as P

HEAD_DIM = 64
BLOCK = 128
GLOBALS = 256
RAND = 3
SPREAD = 2
TOK = 256
FEATS = 256
HEADS_HERE = FEATS // HEAD_DIM
LOG2_SCALE = math.log2(math.e) / math.sqrt(HEAD_DIM)
NEG = -1e30
VMEM_LIMIT = 67043328
MESH = pl.DeviceIdType.MESH
F32 = jnp.float32
BF16 = jnp.bfloat16


def dot_nn(a, b):
    return jnp.dot(a, b, preferred_element_type=F32)


def dot_nt(a, b):
    return lax.dot_general(a, b, (((1,), (1,)), ((), ())), preferred_element_type=F32)


def split_of(shards):
    return {128: (4, 4, 4), 32: (4, 2, 2)}[shards]


def scratch_of(split, heads, d):
    y_n, zn_n, zf_n = split
    r = 2 * y_n
    ch = GLOBALS // r
    qc = GLOBALS // y_n
    piece = 2 * FEATS // zn_n
    vm = pltpu.VMEM
    out = {
        "tok": vm((TOK, d), BF16),
        "wq": vm((d, FEATS), BF16),
        "wk": vm((d, FEATS), BF16),
        "wv": vm((d, FEATS), BF16),
        "osl": vm((heads, FEATS, d), BF16),
        "asl": vm((heads - 1, TOK // heads, FEATS), BF16),
        "att": vm((TOK, FEATS), BF16),
        "attl": vm((TOK, FEATS), F32),
        "att_t": vm((FEATS, TOK), F32),
        "q": vm((TOK, FEATS), BF16),
        "kx": vm((10, BLOCK, FEATS), BF16),
        "vx": vm((10, FEATS, BLOCK), BF16),
        "gvt": vm((2, FEATS, BLOCK), BF16),
        "s": vm((7, BLOCK, 2 * BLOCK), F32),
        "peak": vm((4, 1, 2 * BLOCK), F32),
        "total": vm((4, 1, 2 * BLOCK), F32),
        "acc": vm((4, 2 * HEAD_DIM, 2 * BLOCK), F32),
        "pick": vm((TOK, GLOBALS), BF16),
        "kg": vm((r, 2, BLOCK, 2 * HEAD_DIM), BF16),
        "vg": vm((r, 2, 2 * HEAD_DIM, BLOCK), BF16),
        "s2": vm((r, 2 * BLOCK, 2 * qc), F32),
        "q_part": vm((GLOBALS, FEATS), BF16),
        "q_a": vm((r - 1, qc, 2 * HEAD_DIM), BF16),
        "q_bs": vm((qc, 2 * HEAD_DIM), BF16),
        "q_b": vm((zn_n - 1, qc, 2 * HEAD_DIM), BF16),
        "q_cs": vm((qc, 2 * HEAD_DIM), BF16),
        "q_c": vm((zf_n - 1, qc, 2 * HEAD_DIM), BF16),
        "kv_part": vm((GLOBALS, 2 * FEATS), BF16),
        "kv_a": vm((r - 1, ch, 2 * FEATS), BF16),
        "kv_bs": vm((ch, 2 * FEATS), BF16),
        "kv_b": vm((zn_n - 1, ch, piece), BF16),
        "kv_cs": vm((ch, piece), BF16),
        "kv_c": vm((zf_n - 1, ch, piece), BF16),
        "kv_full": vm((GLOBALS, 2 * FEATS), BF16),
        "o_bs": vm((HEAD_DIM, 2 * qc), BF16),
        "o_b": vm((zn_n - 1, HEAD_DIM, 2 * qc), BF16),
        "o_cs": vm((HEAD_DIM, 2 * qc), BF16),
        "o_c": vm((zf_n - 1, HEAD_DIM, 2 * qc), BF16),
        "o_full": vm((GLOBALS, FEATS), BF16),
        "l_bs": vm((1, 2 * qc), F32),
        "l_b": vm((zn_n - 1, 1, 2 * qc), F32),
        "l_cs": vm((1, 2 * qc), F32),
        "l_c": vm((zf_n - 1, 1, 2 * qc), F32),
        "grow": vm((1, GLOBALS), jnp.int32),
        "rand": pltpu.SMEM((2, RAND), jnp.int32),
    }
    z_copies = zn_n + zf_n - 2
    copies = 3 * (r - 1) + 4 * z_copies + (r - 1) + (zn_n - 1) + 12 + 8 + 2 * (heads - 1)
    out["send"] = pltpu.SemaphoreType.DMA((copies,))
    out["recv"] = pltpu.SemaphoreType.DMA((copies,))
    out["load"] = pltpu.SemaphoreType.DMA((7,))
    return out


def kernel(split, heads, names, tok_h, wq_h, wk_h, wv_h, ow_h, rand_h, grow_h, out_v, *scratch):
    m = dict(zip(names, scratch))
    y_n, zn_n, zf_n = split
    r = 2 * y_n
    ch = GLOBALS // r
    qc = GLOBALS // y_n
    piece = 2 * FEATS // zn_n
    half = 2 * HEAD_DIM
    shards = r * zn_n * zf_n
    z_n = zn_n * zf_n
    tm = lax.axis_index("tm")
    hd = lax.axis_index("head")

    order = (("grow", grow_h), ("tok", tok_h), ("wq", wq_h), ("wk", wk_h), ("wv", wv_h))
    order += (("osl", ow_h), ("rand", rand_h))
    loads = {}
    for i, (name, src) in enumerate(order):
        dst = m[name].at[0] if name == "osl" else m[name]
        loads[name] = pltpu.make_async_copy(src, dst, m["load"].at[i])
        loads[name].start()

    y = tm // (2 * z_n)
    z = (tm // 2) % z_n
    c = tm % 2
    j = y * 2 + c
    zn = z % zn_n
    zf = z // zn_n

    def dev_yc(yy, cc):
        return (yy * (2 * z_n) + z * 2 + cc, hd)

    def dev_z(zz):
        return (y * (2 * z_n) + zz * 2 + c, hd)

    steps_j = [(2, 0), (2, 1), (1, 0), (1, 1), (3, 0), (3, 1), (0, 1)]
    there = [((y + dy) % y_n, (c + e) % 2) for dy, e in steps_j]
    group_j = [dev_yc(*at) for at in there]
    near = [(zn + d) % zn_n for d in range(1, zn_n)]
    group_n = [dev_z(zf * zn_n + at) for at in near]
    far_steps = sorted(range(1, zf_n), key=lambda d: -min(d, zf_n - d))
    group_f = [dev_z(((zf + d) % zf_n) * zn_n + zn) for d in far_steps]
    group_h = [(tm, (hd + d) % heads) for d in range(1, heads)]
    steps_w = (2, -2, 1, -1)
    group_w = [((tm + d + shards) % shards, hd) for d in steps_w]
    everyone = group_j + group_n + group_f + group_h + group_w

    barrier = pltpu.get_barrier_semaphore()
    for dev in everyone:
        pl.semaphore_signal(barrier, inc=1, device_id=dev, device_id_type=MESH)

    count = [0]
    started = []

    def send(src, dst, dev):
        n = count[0]
        count[0] += 1
        copy = pltpu.make_async_remote_copy(
            src_ref=src,
            dst_ref=dst,
            send_sem=m["send"].at[n],
            recv_sem=m["recv"].at[n],
            device_id=dev,
            device_id_type=MESH,
        )
        copy.start()
        started.append(copy)
        return copy

    def part_of(at, size):
        return pl.ds(pl.multiple_of(at * size, size), size)

    def gather(first, copies, slots):
        total = first.astype(F32)
        for n, copy in enumerate(copies):
            copy.wait_recv()
            total = total + slots[n].astype(F32)
        return total.astype(BF16)

    def to_all(src, dst, group):
        return [send(src, dst.at[n], dev) for n, dev in enumerate(group)]

    loads["grow"].wait()
    spots = lax.broadcasted_iota(jnp.int32, (TOK, GLOBALS), 0) + tm * TOK
    pick = jnp.where(spots == m["grow"][...], 1.0, 0.0).astype(F32)
    m["pick"][...] = pick.astype(BF16)
    pick_t = pick.T.astype(BF16)
    loads["tok"].wait()
    loads["wq"].wait()
    q = dot_nn(m["tok"][...], m["wq"][...]).astype(BF16)
    m["q"][...] = q
    m["q_part"][...] = dot_nn(pick_t, q).astype(BF16)
    pl.semaphore_wait(barrier, len(everyone))
    qa = [
        send(m["q_part"].at[part_of(yy, qc), part_of(cc, half)], m["q_a"].at[n], group_j[n])
        for n, (yy, cc) in enumerate(there)
    ]

    loads["wk"].wait()
    k = dot_nn(m["tok"][...], m["wk"][...]).astype(BF16)
    m["kv_part"][:, :FEATS] = dot_nn(pick_t, k).astype(BF16)
    for b in range(2):
        m["kx"][4 + b] = k[b * BLOCK : (b + 1) * BLOCK]
    loads["wv"].wait()
    v32 = dot_nn(m["tok"][...], m["wv"][...])
    m["kv_part"][:, FEATS:] = dot_nn(pick_t, v32.astype(BF16)).astype(BF16)
    kva = [
        send(m["kv_part"].at[part_of(yy * 2 + cc, ch)], m["kv_a"].at[n], group_j[n])
        for n, (yy, cc) in enumerate(there)
    ]
    v_t = v32.T.astype(BF16)
    for b in range(2):
        m["vx"][4 + b] = v_t[:, b * BLOCK : (b + 1) * BLOCK]

    kg_in, vg_in = {}, {}
    for (dy, e), (yy, cc), dev in zip(steps_j, there, group_j):
        if dy == 2:
            continue
        slot = ((y_n - dy) % y_n) * 2 + e
        kg_in[(dy, e)] = send(m["kx"].at[pl.ds(4, 2), :, part_of(cc, half)], m["kg"].at[slot], dev)
        vg_in[(dy, e)] = send(m["vx"].at[pl.ds(4, 2), part_of(cc, half), :], m["vg"].at[slot], dev)

    def start_window(name):
        return [
            send(m[name].at[pl.ds(4, 2)], m[name].at[pl.ds(2 * (SPREAD - step), 2)], dev)
            for step, dev in zip(steps_w, group_w)
        ]

    window = start_window("kx")
    loads["osl"].wait()
    ow = [send(m["osl"].at[0], m["osl"].at[d + 1], group_h[d]) for d in range(heads - 1)]
    for b in range(2):
        m["kg"][0, b] = m["kx"][4 + b, :, part_of(c, half)]
        m["vg"][0, b] = m["vx"][4 + b, part_of(c, half), :]

    m["q_bs"][...] = gather(m["q_part"][part_of(y, qc), part_of(c, half)], qa, m["q_a"])
    qb = to_all(m["q_bs"], m["q_b"], group_n)
    m["kv_bs"][...] = gather(m["kv_part"][part_of(j, ch), :], kva, m["kv_a"])
    kvb = [
        send(m["kv_bs"].at[:, part_of(at, piece)], m["kv_b"].at[n], group_n[n])
        for n, at in enumerate(near)
    ]
    m["q_cs"][...] = gather(m["q_bs"][...], qb, m["q_b"])
    qcs = to_all(m["q_cs"], m["q_c"], group_f)
    m["kv_cs"][...] = gather(m["kv_bs"][:, part_of(zn, piece)], kvb, m["kv_b"])
    kvc = to_all(m["kv_cs"], m["kv_c"], group_f)
    window += start_window("vx")

    for e in range(2):
        kg_in.pop((1, e)).wait_recv()
    forward = [send(m["kg"].at[pl.ds(6, 2)], m["kg"].at[pl.ds(4, 2)], group_j[2])]
    for e in range(2):
        vg_in.pop((3, e)).wait_recv()
    forward += [send(m["vg"].at[pl.ds(2, 2)], m["vg"].at[pl.ds(4, 2)], group_j[4])]

    gq = gather(m["q_cs"][...], qcs, m["q_c"])
    for copy in list(kg_in.values()) + list(vg_in.values()) + forward:
        copy.wait_recv()

    def head_mask(h, width):
        lane_head = lax.broadcasted_iota(jnp.int32, (1, width), 1) // HEAD_DIM
        return jnp.where(lane_head == h, 1.0, 0.0).astype(BF16)

    gq2 = jnp.concatenate([gq * head_mask(0, half), gq * head_mask(1, half)], axis=0)
    peak = None
    for n in range(r):
        s = dot_nt(m["kg"][n].reshape(2 * BLOCK, half), gq2) * LOG2_SCALE
        m["s2"][n] = s
        top = jnp.max(s, axis=0, keepdims=True)
        peak = top if peak is None else jnp.maximum(peak, top)
    total = jnp.zeros((1, 2 * qc), F32)
    acc = jnp.zeros((half, 2 * qc), F32)
    for n in range(r):
        e = jnp.exp2(m["s2"][n] - peak)
        total = total + jnp.sum(e, axis=0, keepdims=True)
        e = e.astype(BF16)
        acc = acc + dot_nn(m["vg"][n, 0], e[:BLOCK]) + dot_nn(m["vg"][n, 1], e[BLOCK:])
    first = lax.broadcasted_iota(jnp.int32, (1, 2 * qc), 1) < qc
    acc = jnp.where(first, acc[:HEAD_DIM], acc[HEAD_DIM:])
    m["o_bs"][...] = (acc / total).astype(BF16)
    m["l_bs"][...] = peak + jnp.log2(total)

    def combine(tag, copies):
        for copy in copies:
            copy.wait_recv()
        slots = "b" if tag == "bs" else "c"
        size = len(copies) // 2
        logs = [m["l_" + tag][...]] + [m["l_" + slots][n] for n in range(size)]
        peak = functools.reduce(jnp.maximum, logs)
        shares = [jnp.exp2(x - peak) for x in logs]
        total = functools.reduce(jnp.add, shares)
        acc = m["o_" + tag][...].astype(F32) * shares[0]
        for n in range(size):
            acc = acc + m["o_" + slots][n].astype(F32) * shares[n + 1]
        return acc / total, peak + jnp.log2(total)

    ob = to_all(m["o_bs"], m["o_b"], group_n) + to_all(m["l_bs"], m["l_b"], group_n)

    mine = m["kv_full"].at[part_of(j, ch), part_of(zn, piece)]
    m["kv_full"][part_of(j, ch), part_of(zn, piece)] = gather(m["kv_cs"][...], kvc, m["kv_c"])
    kve = [send(mine, mine, dev) for dev in group_n]

    o, l = combine("bs", ob)
    m["o_cs"][...] = o.astype(BF16)
    m["l_cs"][...] = l
    oc = to_all(m["o_cs"], m["o_c"], group_f) + to_all(m["l_cs"], m["l_c"], group_f)

    for copy in kve:
        copy.wait_recv()
    mine = m["kv_full"].at[part_of(j, ch), :]
    kvd = [send(mine, mine, dev) for dev in group_j]

    loads["rand"].wait()
    for copy in window:
        copy.wait_recv()
    blocks = 2 * shards

    def queries_of(jb, pair):
        qb_here = m["q"][part_of(jb, BLOCK), :]
        return jnp.concatenate(
            [qb_here * head_mask(2 * pair, FEATS), qb_here * head_mask(2 * pair + 1, FEATS)],
            axis=0,
        )

    def attend_near(step, carry):
        jb = step // 2
        pair = step % 2
        q2 = queries_of(jb, pair)
        feats = part_of(pair, half)
        spots_x = [2 + jb + w for w in range(4)]
        spots_x += [
            jnp.clip(m["rand"][jb, n] - 2 * tm + 2 * SPREAD, 0, 9) for n in range(RAND)
        ]
        peak = None
        for n in range(7):
            s = dot_nt(m["kx"][spots_x[n]], q2) * LOG2_SCALE
            if n in (0, 1, 3):
                block = 2 * tm + jb + n - 2
                inside = (block >= 0) & (block < blocks)
                s = jnp.where(inside, s, NEG)
            m["s"][n] = s
            top = jnp.max(s, axis=0, keepdims=True)
            peak = top if peak is None else jnp.maximum(peak, top)
        total = jnp.zeros((1, 2 * BLOCK), F32)
        acc = jnp.zeros((half, 2 * BLOCK), F32)
        for n in range(7):
            e = jnp.exp2(m["s"][n] - peak)
            total = total + jnp.sum(e, axis=0, keepdims=True)
            acc = acc + dot_nn(m["vx"][spots_x[n], feats, :], e.astype(BF16))
        m["peak"][step] = peak
        m["total"][step] = total
        m["acc"][step] = acc
        return carry

    lax.fori_loop(0, 4, attend_near, 0)

    for copy in kvd:
        copy.wait_recv()
    gv_t = m["kv_full"][:, FEATS:].astype(F32).T.astype(BF16)
    for b in range(2):
        m["gvt"][b] = gv_t[:, b * BLOCK : (b + 1) * BLOCK]

    def attend_global(step, carry):
        jb = step // 2
        pair = step % 2
        q2 = queries_of(jb, pair)
        feats = part_of(pair, half)
        s = dot_nt(m["kv_full"][:, :FEATS], q2) * LOG2_SCALE
        before = m["peak"][step]
        peak = jnp.maximum(before, jnp.max(s, axis=0, keepdims=True))
        e = jnp.exp2(s - peak)
        share = jnp.exp2(before - peak)
        total = m["total"][step] * share + jnp.sum(e, axis=0, keepdims=True)
        e = e.astype(BF16)
        acc = m["acc"][step] * share
        for b in range(2):
            acc = acc + dot_nn(m["gvt"][b, feats, :], e[b * BLOCK : (b + 1) * BLOCK])
        acc = acc / total
        for n in range(2):
            m["att_t"][part_of(pair * 2 + n, HEAD_DIM), part_of(jb, BLOCK)] = acc[
                n * HEAD_DIM : (n + 1) * HEAD_DIM, n * BLOCK : (n + 1) * BLOCK
            ]
        return carry

    lax.fori_loop(0, 4, attend_global, 0)
    is_global = jnp.max(m["pick"][...].astype(F32), axis=1, keepdims=True)
    m["attl"][...] = jnp.where(is_global > 0.5, 0.0, m["att_t"][...].T)

    o, _ = combine("cs", oc)
    o_t = o.T
    o_t = jnp.concatenate([o_t[:qc], o_t[qc:]], axis=1).astype(BF16)
    m["o_full"][part_of(y, qc), part_of(c, half)] = o_t
    mine = m["o_full"].at[part_of(y, qc), part_of(c, half)]
    od = [send(mine, mine, dev) for dev in group_j]
    for copy in od:
        copy.wait_recv()

    placed = dot_nn(m["pick"][...], m["o_full"][...])
    m["att"][...] = (placed + m["attl"][...]).astype(BF16)
    per = TOK // heads
    ax = [
        send(m["att"].at[part_of((hd + d + 1) % heads, per)], m["asl"].at[d], group_h[d])
        for d in range(heads - 1)
    ]
    mixed = dot_nn(m["att"][part_of(hd, per)], m["osl"][0])
    for d in range(heads - 1):
        ow[d].wait_recv()
        ax[d].wait_recv()
        mixed = mixed + dot_nn(m["asl"][d], m["osl"][d + 1])
    out_v[...] = mixed.astype(BF16)
    for copy in started:
        copy.wait_send()


def shards_fn(tokens, q_weight, k_weight, v_weight, o_weight, rand_blocks, global_pos):
    shards = lax.axis_size("tm")
    heads = lax.axis_size("head")
    split = split_of(shards)
    d = tokens.shape[1]
    scratch = scratch_of(split, heads, d)
    hbm = pl.BlockSpec(memory_space=pl.ANY)
    return pl.pallas_call(
        functools.partial(kernel, split, heads, list(scratch)),
        out_shape=jax.ShapeDtypeStruct((TOK // heads, d), BF16),
        in_specs=[hbm] * 7,
        out_specs=pl.BlockSpec(memory_space=pltpu.VMEM),
        scratch_shapes=list(scratch.values()),
        compiler_params=pltpu.CompilerParams(
            collective_id=0, has_side_effects=True, vmem_limit_bytes=VMEM_LIMIT
        ),
        name="layer",
    )(
        tokens,
        q_weight,
        k_weight,
        v_weight,
        o_weight,
        rand_blocks,
        global_pos.reshape(1, GLOBALS),
    )


def solution(mesh):
    placed = (
        P("tm", None),
        P(None, "head"),
        P(None, "head"),
        P(None, "head"),
        P("head", None),
        P("tm", None),
        P(),
    )
    return jax.shard_map(
        shards_fn, mesh=mesh, in_specs=placed, out_specs=P(("tm", "head"), None), check_vma=False
    )
```

```python
import functools
import math

import jax
import jax.numpy as jnp
from jax import lax
from jax.experimental import pallas as pl
from jax.experimental.pallas import tpu as pltpu
from jax.sharding import PartitionSpec as P

HEAD_DIM = 64
BLOCK = 128
GLOBALS = 256
RAND = 3
SPREAD = 2
TOK = 256
FEATS = 256
HEADS_HERE = FEATS // HEAD_DIM
LOG2_SCALE = math.log2(math.e) / math.sqrt(HEAD_DIM)
NEG = -1e30
VMEM_LIMIT = 56000000
MESH = pl.DeviceIdType.MESH
F32 = jnp.float32
BF16 = jnp.bfloat16


def dot_nn(a, b):
    return jnp.dot(a, b, preferred_element_type=F32)


def dot_nt(a, b):
    return lax.dot_general(a, b, (((1,), (1,)), ((), ())), preferred_element_type=F32)


def split_of(shards):
    return {128: (4, 4, 4), 32: (4, 2, 2)}[shards]


def scratch_of(split, heads, d):
    y_n, zn_n, zf_n = split
    r = 2 * y_n
    ch = GLOBALS // r
    qc = GLOBALS // y_n
    piece = 2 * FEATS // zn_n
    vm = pltpu.VMEM
    out = {
        "tok": vm((TOK, d), BF16),
        "wq": vm((d, FEATS), BF16),
        "wk": vm((d, FEATS), BF16),
        "wv": vm((d, FEATS), BF16),
        "osl": vm((heads, FEATS, d), BF16),
        "asl": vm((heads - 1, TOK // heads, FEATS), BF16),
        "att": vm((TOK, FEATS), BF16),
        "attl": vm((TOK, FEATS), F32),
        "att_t": vm((FEATS, TOK), F32),
        "q": vm((TOK, FEATS), BF16),
        "kx": vm((10, BLOCK, FEATS), BF16),
        "vx": vm((10, FEATS, BLOCK), BF16),
        "gvt": vm((2, FEATS, BLOCK), BF16),
        "s": vm((7, BLOCK, 2 * BLOCK), F32),
        "peak": vm((4, 1, 2 * BLOCK), F32),
        "total": vm((4, 1, 2 * BLOCK), F32),
        "acc": vm((4, 2 * HEAD_DIM, 2 * BLOCK), F32),
        "pick": vm((TOK, GLOBALS), BF16),
        "kg": vm((r, 2, BLOCK, 2 * HEAD_DIM), BF16),
        "vg": vm((r, 2, 2 * HEAD_DIM, BLOCK), BF16),
        "s2": vm((r, 2 * BLOCK, 2 * qc), F32),
        "q_part": vm((GLOBALS, FEATS), BF16),
        "q_a": vm((r - 1, qc, 2 * HEAD_DIM), BF16),
        "q_bs": vm((qc, 2 * HEAD_DIM), BF16),
        "q_b": vm((zn_n - 1, qc, 2 * HEAD_DIM), BF16),
        "q_cs": vm((qc, 2 * HEAD_DIM), BF16),
        "q_c": vm((zf_n - 1, qc, 2 * HEAD_DIM), BF16),
        "kv_part": vm((GLOBALS, 2 * FEATS), BF16),
        "kv_a": vm((r - 1, ch, 2 * FEATS), BF16),
        "kv_bs": vm((ch, 2 * FEATS), BF16),
        "kv_b": vm((zn_n - 1, ch, piece), BF16),
        "kv_cs": vm((ch, piece), BF16),
        "kv_c": vm((zf_n - 1, ch, piece), BF16),
        "kv_full": vm((GLOBALS, 2 * FEATS), BF16),
        "o_bs": vm((HEAD_DIM, 2 * qc), BF16),
        "o_b": vm((zn_n - 1, HEAD_DIM, 2 * qc), BF16),
        "o_cs": vm((HEAD_DIM, 2 * qc), BF16),
        "o_c": vm((zf_n - 1, HEAD_DIM, 2 * qc), BF16),
        "o_full": vm((GLOBALS, FEATS), BF16),
        "l_bs": vm((1, 2 * qc), F32),
        "l_b": vm((zn_n - 1, 1, 2 * qc), F32),
        "l_cs": vm((1, 2 * qc), F32),
        "l_c": vm((zf_n - 1, 1, 2 * qc), F32),
        "grow": vm((1, GLOBALS), jnp.int32),
        "rand": pltpu.SMEM((2, RAND), jnp.int32),
    }
    z_copies = zn_n + zf_n - 2
    copies = 3 * (r - 1) + 4 * z_copies + (r - 1) + (zn_n - 1) + 2 * (r - 2) + 8 + 2 * (heads - 1)
    out["send"] = pltpu.SemaphoreType.DMA((copies,))
    out["recv"] = pltpu.SemaphoreType.DMA((copies,))
    out["greet"] = pltpu.SemaphoreType.REGULAR
    out["load"] = pltpu.SemaphoreType.DMA((7,))
    return out


def kernel(split, heads, names, tok_h, wq_h, wk_h, wv_h, ow_h, rand_h, grow_h, out_v, *scratch):
    m = dict(zip(names, scratch))
    y_n, zn_n, zf_n = split
    r = 2 * y_n
    ch = GLOBALS // r
    qc = GLOBALS // y_n
    piece = 2 * FEATS // zn_n
    half = 2 * HEAD_DIM
    shards = r * zn_n * zf_n
    z_n = zn_n * zf_n
    tm = lax.axis_index("tm")
    hd = lax.axis_index("head")

    order = (("grow", grow_h), ("tok", tok_h), ("wq", wq_h), ("wk", wk_h), ("wv", wv_h))
    order += (("osl", ow_h), ("rand", rand_h))
    loads = {}
    for i, (name, src) in enumerate(order):
        dst = m[name].at[0] if name == "osl" else m[name]
        loads[name] = pltpu.make_async_copy(src, dst, m["load"].at[i])
        loads[name].start()

    y = tm // (2 * z_n)
    z = (tm // 2) % z_n
    c = tm % 2
    j = y * 2 + c
    zn = z % zn_n
    zf = z // zn_n

    def dev_yc(yy, cc):
        return (yy * (2 * z_n) + z * 2 + cc, hd)

    def dev_z(zz):
        return (y * (2 * z_n) + zz * 2 + c, hd)

    steps_j = [(2, 0), (2, 1), (1, 0), (1, 1), (3, 0), (3, 1), (0, 1)]
    there = [((y + dy) % y_n, (c + e) % 2) for dy, e in steps_j]
    group_j = [dev_yc(*at) for at in there]
    near = [(zn + d) % zn_n for d in range(1, zn_n)]
    group_n = [dev_z(zf * zn_n + at) for at in near]
    far_steps = sorted(range(1, zf_n), key=lambda d: -min(d, zf_n - d))
    group_f = [dev_z(((zf + d) % zf_n) * zn_n + zn) for d in far_steps]
    group_h = [(tm, (hd + d) % heads) for d in range(1, heads)]
    steps_w = (2, -2)
    partner = dev_yc(y, 1 - c)
    group_w = [((tm + d + shards) % shards, hd) for d in steps_w]
    next_f = [dev for d, dev in zip(far_steps, group_f) if min(d, zf_n - d) == 1]
    relayed = len(next_f) < len(group_f)
    everyone = group_j + group_n + next_f + group_h + group_w

    barrier = pltpu.get_barrier_semaphore()
    for dev in everyone:
        pl.semaphore_signal(barrier, inc=1, device_id=dev, device_id_type=MESH)

    count = [0]
    started = []

    def plan(src, dst, dev):
        n = count[0]
        count[0] += 1
        copy = pltpu.make_async_remote_copy(
            src_ref=src,
            dst_ref=dst,
            send_sem=m["send"].at[n],
            recv_sem=m["recv"].at[n],
            device_id=dev,
            device_id_type=MESH,
        )
        started.append(copy)
        return copy

    def send(src, dst, dev):
        copy = plan(src, dst, dev)
        copy.start()
        return copy

    def part_of(at, size):
        return pl.ds(pl.multiple_of(at * size, size), size)

    def gather(first, copies, slots):
        total = first.astype(F32)
        for n, copy in enumerate(copies):
            copy.wait_recv()
            total = total + slots[n].astype(F32)
        return total.astype(BF16)

    def to_all(src, dst, group):
        return [send(src, dst.at[n], dev) for n, dev in enumerate(group)]

    loads["grow"].wait()
    spots = lax.broadcasted_iota(jnp.int32, (TOK, GLOBALS), 0) + tm * TOK
    pick = jnp.where(spots == m["grow"][...], 1.0, 0.0).astype(F32)
    m["pick"][...] = pick.astype(BF16)
    pick_t = pick.T.astype(BF16)
    loads["tok"].wait()
    loads["wq"].wait()
    q = dot_nn(m["tok"][...], m["wq"][...]).astype(BF16)
    m["q"][...] = q
    m["q_part"][...] = dot_nn(pick_t, q).astype(BF16)
    pl.semaphore_wait(barrier, len(everyone))
    if relayed:
        for dev in next_f:
            pl.semaphore_signal(m["greet"], inc=1, device_id=dev, device_id_type=MESH)
    qa = [
        send(m["q_part"].at[part_of(yy, qc), part_of(cc, half)], m["q_a"].at[n], group_j[n])
        for n, (yy, cc) in enumerate(there)
    ]

    loads["wk"].wait()
    k = dot_nn(m["tok"][...], m["wk"][...]).astype(BF16)
    m["kv_part"][:, :FEATS] = dot_nn(pick_t, k).astype(BF16)
    for b in range(2):
        m["kx"][4 + b] = k[b * BLOCK : (b + 1) * BLOCK]
    loads["wv"].wait()
    v32 = dot_nn(m["tok"][...], m["wv"][...])
    m["kv_part"][:, FEATS:] = dot_nn(pick_t, v32.astype(BF16)).astype(BF16)
    kva = [
        send(m["kv_part"].at[part_of(yy * 2 + cc, ch)], m["kv_a"].at[n], group_j[n])
        for n, (yy, cc) in enumerate(there)
    ]
    v_t = v32.T.astype(BF16)
    for b in range(2):
        m["vx"][4 + b] = v_t[:, b * BLOCK : (b + 1) * BLOCK]


    edges = (z == z_n - 1, z == 0)
    window, beside = [], []
    for name in ("kx", "vx"):
        own = m[name].at[pl.ds(4, 2)]
        for step, dev in zip(steps_w, group_w):
            window.append(plan(own, m[name].at[pl.ds(2 * (SPREAD - step), 2)], dev))
        beside.append(send(own, m[name].at[pl.ds(2 + 4 * c, 2)], partner))

    def start_window(copies, at_edge):
        for n, copy in enumerate(copies):
            pl.when(edges[n % 2] if at_edge else jnp.logical_not(edges[n % 2]))(copy.start)

    start_window(window[:2], False)
    loads["osl"].wait()
    ow = [send(m["osl"].at[0], m["osl"].at[d + 1], group_h[d]) for d in range(heads - 1)]
    for b in range(2):
        m["kg"][0, b] = m["kx"][4 + b, :, part_of(c, half)]
        m["vg"][0, b] = m["vx"][4 + b, part_of(c, half), :]

    m["q_bs"][...] = gather(m["q_part"][part_of(y, qc), part_of(c, half)], qa, m["q_a"])
    qb = to_all(m["q_bs"], m["q_b"], group_n)
    kg_in, vg_in = {}, {}
    for (dy, e), (yy, cc), dev in zip(steps_j, there, group_j):
        if dy == 2:
            continue
        slot = ((y_n - dy) % y_n) * 2 + e
        ks = m["kx"].at[pl.ds(4, 2), :, part_of(cc, half)]
        vs = m["vx"].at[pl.ds(4, 2), part_of(cc, half), :]
        ways = [(kg_in, ks, "kg"), (vg_in, vs, "vg")]
        for way, src, name in ways if dy == 1 else ways[::-1]:
            way[(dy, e)] = send(src, m[name].at[slot], dev)
    m["kv_bs"][...] = gather(m["kv_part"][part_of(j, ch), :], kva, m["kv_a"])
    kvb = [
        send(m["kv_bs"].at[:, part_of(at, piece)], m["kv_b"].at[n], group_n[n])
        for n, at in enumerate(near)
    ]
    m["q_cs"][...] = gather(m["q_bs"][...], qb, m["q_b"])
    if relayed:
        pl.semaphore_wait(m["greet"], len(next_f))
    qcs = to_all(m["q_cs"], m["q_c"], group_f)
    m["kv_cs"][...] = gather(m["kv_bs"][:, part_of(zn, piece)], kvb, m["kv_b"])
    kvc = to_all(m["kv_cs"], m["kv_c"], group_f)
    start_window(window[2:], False)
    for e in range(2):
        kg_in.pop((1, e)).wait_recv()
    forward = [send(m["kg"].at[pl.ds(6, 2)], m["kg"].at[pl.ds(4, 2)], group_j[2])]
    for e in range(2):
        vg_in.pop((3, e)).wait_recv()
    forward += [send(m["vg"].at[pl.ds(2, 2)], m["vg"].at[pl.ds(4, 2)], group_j[4])]
    gq = gather(m["q_cs"][...], qcs, m["q_c"])
    start_window(window, True)
    mine = m["kv_full"].at[part_of(j, ch), part_of(zn, piece)]
    m["kv_full"][part_of(j, ch), part_of(zn, piece)] = gather(m["kv_cs"][...], kvc, m["kv_c"])
    kve = [send(mine, mine, dev) for dev in group_n]

    for copy in list(kg_in.values()) + list(vg_in.values()) + forward:
        copy.wait_recv()

    def head_mask(h, width):
        lane_head = lax.broadcasted_iota(jnp.int32, (1, width), 1) // HEAD_DIM
        return jnp.where(lane_head == h, 1.0, 0.0).astype(BF16)

    gq2 = jnp.concatenate([gq * head_mask(0, half), gq * head_mask(1, half)], axis=0)
    peak = None
    for n in range(r):
        s = dot_nt(m["kg"][n].reshape(2 * BLOCK, half), gq2) * LOG2_SCALE
        m["s2"][n] = s
        top = jnp.max(s, axis=0, keepdims=True)
        peak = top if peak is None else jnp.maximum(peak, top)
    total = jnp.zeros((1, 2 * qc), F32)
    acc = jnp.zeros((half, 2 * qc), F32)
    for n in range(r):
        e = jnp.exp2(m["s2"][n] - peak)
        total = total + jnp.sum(e, axis=0, keepdims=True)
        e = e.astype(BF16)
        acc = acc + dot_nn(m["vg"][n, 0], e[:BLOCK]) + dot_nn(m["vg"][n, 1], e[BLOCK:])
    first = lax.broadcasted_iota(jnp.int32, (1, 2 * qc), 1) < qc
    acc = jnp.where(first, acc[:HEAD_DIM], acc[HEAD_DIM:])
    m["o_bs"][...] = (acc / total).astype(BF16)
    m["l_bs"][...] = peak + jnp.log2(total)

    def combine(tag, copies):
        for copy in copies:
            copy.wait_recv()
        slots = "b" if tag == "bs" else "c"
        size = len(copies) // 2
        logs = [m["l_" + tag][...]] + [m["l_" + slots][n] for n in range(size)]
        peak = functools.reduce(jnp.maximum, logs)
        shares = [jnp.exp2(x - peak) for x in logs]
        total = functools.reduce(jnp.add, shares)
        acc = m["o_" + tag][...].astype(F32) * shares[0]
        for n in range(size):
            acc = acc + m["o_" + slots][n].astype(F32) * shares[n + 1]
        return acc / total, peak + jnp.log2(total)

    ob = to_all(m["o_bs"], m["o_b"], group_n) + to_all(m["l_bs"], m["l_b"], group_n)

    for copy in kve:
        copy.wait_recv()
    mine = m["kv_full"].at[part_of(j, ch), :]
    kvd = [send(mine, mine, dev) for dev in group_j]

    o, l = combine("bs", ob)
    m["o_cs"][...] = o.astype(BF16)
    m["l_cs"][...] = l
    oc = to_all(m["o_cs"], m["o_c"], group_f) + to_all(m["l_cs"], m["l_c"], group_f)

    for copy in window:
        copy.wait_recv()
    for name in ("kx", "vx"):
        beside.append(
            send(m[name].at[pl.ds(8 - 8 * c, 2)], m[name].at[pl.ds(6 - 4 * c, 2)], partner)
        )
    loads["rand"].wait()
    for copy in beside:
        copy.wait_recv()
    blocks = 2 * shards

    def queries_of(jb, pair):
        qb_here = m["q"][part_of(jb, BLOCK), :]
        return jnp.concatenate(
            [qb_here * head_mask(2 * pair, FEATS), qb_here * head_mask(2 * pair + 1, FEATS)],
            axis=0,
        )

    def attend_near(step, carry):
        jb = step // 2
        pair = step % 2
        q2 = queries_of(jb, pair)
        feats = part_of(pair, half)
        spots_x = [2 + jb + w for w in range(4)]
        spots_x += [
            jnp.clip(m["rand"][jb, n] - 2 * tm + 2 * SPREAD, 0, 9) for n in range(RAND)
        ]
        peak = None
        for n in range(7):
            s = dot_nt(m["kx"][spots_x[n]], q2) * LOG2_SCALE
            if n in (0, 1, 3):
                block = 2 * tm + jb + n - 2
                inside = (block >= 0) & (block < blocks)
                s = jnp.where(inside, s, NEG)
            m["s"][n] = s
            top = jnp.max(s, axis=0, keepdims=True)
            peak = top if peak is None else jnp.maximum(peak, top)
        total = jnp.zeros((1, 2 * BLOCK), F32)
        acc = jnp.zeros((half, 2 * BLOCK), F32)
        for n in range(7):
            e = jnp.exp2(m["s"][n] - peak)
            total = total + jnp.sum(e, axis=0, keepdims=True)
            acc = acc + dot_nn(m["vx"][spots_x[n], feats, :], e.astype(BF16))
        m["peak"][step] = peak
        m["total"][step] = total
        m["acc"][step] = acc
        return carry

    for step in range(4):
        attend_near(step, 0)

    for copy in kvd:
        copy.wait_recv()
    gv_t = m["kv_full"][:, FEATS:].astype(F32).T.astype(BF16)
    for b in range(2):
        m["gvt"][b] = gv_t[:, b * BLOCK : (b + 1) * BLOCK]

    def attend_global(step, carry):
        jb = step // 2
        pair = step % 2
        q2 = queries_of(jb, pair)
        feats = part_of(pair, half)
        s = dot_nt(m["kv_full"][:, :FEATS], q2) * LOG2_SCALE
        before = m["peak"][step]
        peak = jnp.maximum(before, jnp.max(s, axis=0, keepdims=True))
        e = jnp.exp2(s - peak)
        share = jnp.exp2(before - peak)
        total = m["total"][step] * share + jnp.sum(e, axis=0, keepdims=True)
        e = e.astype(BF16)
        acc = m["acc"][step] * share
        for b in range(2):
            acc = acc + dot_nn(m["gvt"][b, feats, :], e[b * BLOCK : (b + 1) * BLOCK])
        acc = acc / total
        for n in range(2):
            m["att_t"][part_of(pair * 2 + n, HEAD_DIM), part_of(jb, BLOCK)] = acc[
                n * HEAD_DIM : (n + 1) * HEAD_DIM, n * BLOCK : (n + 1) * BLOCK
            ]
        return carry

    for step in range(4):
        attend_global(step, 0)
    is_global = jnp.max(m["pick"][...].astype(F32), axis=1, keepdims=True)
    m["attl"][...] = jnp.where(is_global > 0.5, 0.0, m["att_t"][...].T)

    o, _ = combine("cs", oc)
    o_t = o.T
    o_t = jnp.concatenate([o_t[:qc], o_t[qc:]], axis=1).astype(BF16)
    m["o_full"][part_of(y, qc), part_of(c, half)] = o_t
    mine = m["o_full"].at[part_of(y, qc), part_of(c, half)]
    od = [send(mine, mine, dev) for dev in group_j]
    for copy in od:
        copy.wait_recv()

    placed = dot_nn(m["pick"][...], m["o_full"][...])
    m["att"][...] = (placed + m["attl"][...]).astype(BF16)
    per = TOK // heads
    ax = [
        send(m["att"].at[part_of((hd + d + 1) % heads, per)], m["asl"].at[d], group_h[d])
        for d in range(heads - 1)
    ]
    mixed = dot_nn(m["att"][part_of(hd, per)], m["osl"][0])
    for d in range(heads - 1):
        ow[d].wait_recv()
        ax[d].wait_recv()
        mixed = mixed + dot_nn(m["asl"][d], m["osl"][d + 1])
    out_v[...] = mixed.astype(BF16)
    for copy in started:
        copy.wait_send()


def shards_fn(tokens, q_weight, k_weight, v_weight, o_weight, rand_blocks, global_pos):
    shards = lax.axis_size("tm")
    heads = lax.axis_size("head")
    split = split_of(shards)
    d = tokens.shape[1]
    scratch = scratch_of(split, heads, d)
    hbm = pl.BlockSpec(memory_space=pl.ANY)
    return pl.pallas_call(
        functools.partial(kernel, split, heads, list(scratch)),
        out_shape=jax.ShapeDtypeStruct((TOK // heads, d), BF16),
        in_specs=[hbm] * 7,
        out_specs=pl.BlockSpec(memory_space=pltpu.VMEM),
        scratch_shapes=list(scratch.values()),
        compiler_params=pltpu.CompilerParams(
            collective_id=0, has_side_effects=True, vmem_limit_bytes=VMEM_LIMIT
        ),
        name="layer",
    )(
        tokens,
        q_weight,
        k_weight,
        v_weight,
        o_weight,
        rand_blocks,
        global_pos.reshape(1, GLOBALS),
    )


def solution(mesh):
    placed = (
        P("tm", None),
        P(None, "head"),
        P(None, "head"),
        P(None, "head"),
        P("head", None),
        P("tm", None),
        P(),
    )
    return jax.shard_map(
        shards_fn, mesh=mesh, in_specs=placed, out_specs=P(("tm", "head"), None), check_vma=False
    )
```

```python
import functools
import math

import jax
import jax.numpy as jnp
from jax import lax
from jax.experimental import pallas as pl
from jax.experimental.pallas import tpu as pltpu
from jax.sharding import PartitionSpec as P

HEAD_DIM = 64
BLOCK = 128
GLOBALS = 256
RAND = 3
SPREAD = 2
TOK = 256
FEATS = 256
HEADS_HERE = FEATS // HEAD_DIM
LOG2_SCALE = math.log2(math.e) / math.sqrt(HEAD_DIM)
NEG = -1e30
VMEM_LIMIT = 56000000
MESH = pl.DeviceIdType.MESH
F32 = jnp.float32
BF16 = jnp.bfloat16


def dot_nn(a, b):
    return jnp.dot(a, b, preferred_element_type=F32)


def dot_nt(a, b):
    return lax.dot_general(a, b, (((1,), (1,)), ((), ())), preferred_element_type=F32)


def split_of(shards):
    return {128: (4, 4, 4), 32: (4, 2, 2)}[shards]


class Group:
    def __init__(self, going, coming):
        self.wait_send = going.wait
        self.wait_recv = coming.wait


def scratch_of(split, heads, d):
    y_n, zn_n, zf_n = split
    r = 2 * y_n
    ch = GLOBALS // r
    qc = GLOBALS // y_n
    piece = 2 * FEATS // zn_n
    vm = pltpu.VMEM
    out = {
        "tok": vm((TOK, d), BF16),
        "wq": vm((d, FEATS), BF16),
        "wk": vm((d, FEATS), BF16),
        "wv": vm((d, FEATS), BF16),
        "osl": vm((heads, FEATS, d), BF16),
        "asl": vm((heads - 1, TOK // heads, FEATS), BF16),
        "att": vm((TOK, FEATS), BF16),
        "attl": vm((TOK, FEATS), F32),
        "att_t": vm((FEATS, TOK), F32),
        "q": vm((TOK, FEATS), BF16),
        "kx": vm((10, BLOCK, FEATS), BF16),
        "vx": vm((10, FEATS, BLOCK), BF16),
        "gvt": vm((2, FEATS, BLOCK), BF16),
        "s": vm((7, BLOCK, 2 * BLOCK), F32),
        "peak": vm((4, 1, 2 * BLOCK), F32),
        "total": vm((4, 1, 2 * BLOCK), F32),
        "acc": vm((4, 2 * HEAD_DIM, 2 * BLOCK), F32),
        "pick": vm((TOK, GLOBALS), BF16),
        "kg": vm((r, 2, BLOCK, 2 * HEAD_DIM), BF16),
        "vg": vm((r, 2, 2 * HEAD_DIM, BLOCK), BF16),
        "s2": vm((r, 2 * BLOCK, 2 * qc), F32),
        "q_part": vm((GLOBALS, FEATS), BF16),
        "q_a": vm((r - 1, qc, 2 * HEAD_DIM), BF16),
        "q_bs": vm((qc, 2 * HEAD_DIM), BF16),
        "q_b": vm((zn_n - 1, qc, 2 * HEAD_DIM), BF16),
        "q_cs": vm((qc, 2 * HEAD_DIM), BF16),
        "q_c": vm((zf_n - 1, qc, 2 * HEAD_DIM), BF16),
        "kv_part": vm((GLOBALS, 2 * FEATS), BF16),
        "kv_a": vm((r - 1, ch, 2 * FEATS), BF16),
        "kv_bs": vm((ch, 2 * FEATS), BF16),
        "kv_b": vm((zn_n - 1, ch, piece), BF16),
        "kv_cs": vm((ch, piece), BF16),
        "kv_c": vm((zf_n - 1, ch, piece), BF16),
        "kv_full": vm((GLOBALS, 2 * FEATS), BF16),
        "o_bs": vm((HEAD_DIM, 2 * qc), BF16),
        "o_b": vm((zn_n - 1, HEAD_DIM, 2 * qc), BF16),
        "o_cs": vm((HEAD_DIM, 2 * qc), BF16),
        "o_c": vm((zf_n - 1, HEAD_DIM, 2 * qc), BF16),
        "o_full": vm((GLOBALS, FEATS), BF16),
        "l_bs": vm((1, 2 * qc), F32),
        "l_b": vm((zn_n - 1, 1, 2 * qc), F32),
        "l_cs": vm((1, 2 * qc), F32),
        "l_c": vm((zf_n - 1, 1, 2 * qc), F32),
        "grow": vm((1, GLOBALS), jnp.int32),
        "rand": pltpu.SMEM((2, RAND), jnp.int32),
    }
    copies = 31
    out["send"] = pltpu.SemaphoreType.DMA((copies,))
    out["recv"] = pltpu.SemaphoreType.DMA((copies,))
    out["greet"] = pltpu.SemaphoreType.REGULAR
    out["load"] = pltpu.SemaphoreType.DMA((7,))
    return out


def kernel(split, heads, names, tok_h, wq_h, wk_h, wv_h, ow_h, rand_h, grow_h, out_v, *scratch):
    m = dict(zip(names, scratch))
    y_n, zn_n, zf_n = split
    r = 2 * y_n
    ch = GLOBALS // r
    qc = GLOBALS // y_n
    piece = 2 * FEATS // zn_n
    half = 2 * HEAD_DIM
    shards = r * zn_n * zf_n
    z_n = zn_n * zf_n
    tm = lax.axis_index("tm")
    hd = lax.axis_index("head")

    order = (("grow", grow_h), ("tok", tok_h), ("wq", wq_h), ("wk", wk_h), ("wv", wv_h))
    order += (("osl", ow_h), ("rand", rand_h))
    loads = {}
    for i, (name, src) in enumerate(order):
        dst = m[name].at[0] if name == "osl" else m[name]
        loads[name] = pltpu.make_async_copy(src, dst, m["load"].at[i])
        loads[name].start()

    y = tm // (2 * z_n)
    z = (tm // 2) % z_n
    c = tm % 2
    j = y * 2 + c
    zn = z % zn_n
    zf = z // zn_n

    def dev_yc(yy, cc):
        return (yy * (2 * z_n) + z * 2 + cc, hd)

    def dev_z(zz):
        return (y * (2 * z_n) + zz * 2 + c, hd)

    steps_j = [(2, 0), (2, 1), (1, 0), (1, 1), (3, 0), (3, 1), (0, 1)]
    there = [((y + dy) % y_n, (c + e) % 2) for dy, e in steps_j]
    group_j = [dev_yc(*at) for at in there]
    near = [(zn + d) % zn_n for d in range(1, zn_n)]
    group_n = [dev_z(zf * zn_n + at) for at in near]
    far_steps = sorted(range(1, zf_n), key=lambda d: -min(d, zf_n - d))
    group_f = [dev_z(((zf + d) % zf_n) * zn_n + zn) for d in far_steps]
    group_h = [(tm, (hd + d) % heads) for d in range(1, heads)]
    steps_w = (2, -2)
    partner = dev_yc(y, 1 - c)
    group_w = [((tm + d + shards) % shards, hd) for d in steps_w]
    next_f = [dev for d, dev in zip(far_steps, group_f) if min(d, zf_n - d) == 1]
    relayed = len(next_f) < len(group_f)
    everyone = group_j + group_n + next_f + group_h + group_w

    barrier = pltpu.get_barrier_semaphore()
    for dev in everyone:
        pl.semaphore_signal(barrier, inc=1, device_id=dev, device_id_type=MESH)

    count = [0]
    started = []

    def plan(src, dst, dev):
        n = count[0]
        count[0] += 1
        copy = pltpu.make_async_remote_copy(
            src_ref=src,
            dst_ref=dst,
            send_sem=m["send"].at[n],
            recv_sem=m["recv"].at[n],
            device_id=dev,
            device_id_type=MESH,
        )
        started.append(copy)
        return copy

    def send(src, dst, dev):
        copy = plan(src, dst, dev)
        copy.start()
        return copy

    def send_all(items, like):
        n = count[0]
        count[0] += 1
        for src, dst, dev in items:
            pltpu.make_async_remote_copy(
                src_ref=src,
                dst_ref=dst,
                send_sem=m["send"].at[n],
                recv_sem=m["recv"].at[n],
                device_id=dev,
                device_id_type=MESH,
            ).start()
        group = Group(*(pltpu.make_async_copy(like, like, m[way].at[n]) for way in ("send", "recv")))
        started.append(group)
        return group

    def part_of(at, size):
        return pl.ds(pl.multiple_of(at * size, size), size)

    def gather(first, group, slots):
        group.wait_recv()
        total = first.astype(F32)
        for n in range(slots.shape[0]):
            total = total + slots[n].astype(F32)
        return total.astype(BF16)

    def to_all(src, dst, group):
        return send_all([(src, dst.at[n], dev) for n, dev in enumerate(group)], dst)

    loads["grow"].wait()
    spots = lax.broadcasted_iota(jnp.int32, (TOK, GLOBALS), 0) + tm * TOK
    pick = jnp.where(spots == m["grow"][...], 1.0, 0.0).astype(F32)
    m["pick"][...] = pick.astype(BF16)
    pick_t = pick.T.astype(BF16)
    loads["tok"].wait()
    loads["wq"].wait()
    q = dot_nn(m["tok"][...], m["wq"][...]).astype(BF16)
    m["q"][...] = q
    m["q_part"][...] = dot_nn(pick_t, q).astype(BF16)
    pl.semaphore_wait(barrier, len(everyone))
    if relayed:
        for dev in next_f:
            pl.semaphore_signal(m["greet"], inc=1, device_id=dev, device_id_type=MESH)
    pieces = [m["q_part"].at[part_of(yy, qc), part_of(cc, half)] for yy, cc in there]
    qa = send_all([(src, m["q_a"].at[n], group_j[n]) for n, src in enumerate(pieces)], m["q_a"])

    loads["wk"].wait()
    k = dot_nn(m["tok"][...], m["wk"][...]).astype(BF16)
    m["kv_part"][:, :FEATS] = dot_nn(pick_t, k).astype(BF16)
    for b in range(2):
        m["kx"][4 + b] = k[b * BLOCK : (b + 1) * BLOCK]
    loads["wv"].wait()
    v32 = dot_nn(m["tok"][...], m["wv"][...])
    m["kv_part"][:, FEATS:] = dot_nn(pick_t, v32.astype(BF16)).astype(BF16)
    pieces = [m["kv_part"].at[part_of(yy * 2 + cc, ch)] for yy, cc in there]
    kva = send_all([(src, m["kv_a"].at[n], group_j[n]) for n, src in enumerate(pieces)], m["kv_a"])
    v_t = v32.T.astype(BF16)
    for b in range(2):
        m["vx"][4 + b] = v_t[:, b * BLOCK : (b + 1) * BLOCK]


    edges = (z == z_n - 1, z == 0)
    window, beside = [], []
    for name in ("kx", "vx"):
        own = m[name].at[pl.ds(4, 2)]
        for step, dev in zip(steps_w, group_w):
            window.append(plan(own, m[name].at[pl.ds(2 * (SPREAD - step), 2)], dev))
        beside.append(send(own, m[name].at[pl.ds(2 + 4 * c, 2)], partner))

    def start_window(copies, at_edge):
        for n, copy in enumerate(copies):
            pl.when(edges[n % 2] if at_edge else jnp.logical_not(edges[n % 2]))(copy.start)

    start_window(window[:2], False)
    loads["osl"].wait()
    ow = send_all(
        [(m["osl"].at[0], m["osl"].at[d + 1], dev) for d, dev in enumerate(group_h)],
        m["osl"].at[pl.ds(1, heads - 1)],
    )
    for b in range(2):
        m["kg"][0, b] = m["kx"][4 + b, :, part_of(c, half)]
        m["vg"][0, b] = m["vx"][4 + b, part_of(c, half), :]

    m["q_bs"][...] = gather(m["q_part"][part_of(y, qc), part_of(c, half)], qa, m["q_a"])
    qb = to_all(m["q_bs"], m["q_b"], group_n)
    kvg = {}
    for dy in (1, 3, 0):
        at = [n for n, step in enumerate(steps_j) if step[0] == dy]
        slots = [((y_n - dy) % y_n) * 2 + steps_j[n][1] for n in at]
        ways = [(m["kx"].at[pl.ds(4, 2), :, part_of(there[n][1], half)], "kg") for n in at]
        ways = [ways] + [
            [(m["vx"].at[pl.ds(4, 2), part_of(there[n][1], half), :], "vg") for n in at]
        ]
        for way in ways if dy == 1 else ways[::-1]:
            name = way[0][1]
            kvg[(name, dy)] = send_all(
                [(way[i][0], m[name].at[slots[i]], group_j[n]) for i, n in enumerate(at)],
                m[name].at[pl.ds(0, len(at))],
            )
    m["kv_bs"][...] = gather(m["kv_part"][part_of(j, ch), :], kva, m["kv_a"])
    pieces = [m["kv_bs"].at[:, part_of(at, piece)] for at in near]
    kvb = send_all([(src, m["kv_b"].at[n], group_n[n]) for n, src in enumerate(pieces)], m["kv_b"])
    m["q_cs"][...] = gather(m["q_bs"][...], qb, m["q_b"])
    if relayed:
        pl.semaphore_wait(m["greet"], len(next_f))
    qcs = to_all(m["q_cs"], m["q_c"], group_f)
    m["kv_cs"][...] = gather(m["kv_bs"][:, part_of(zn, piece)], kvb, m["kv_b"])
    kvc = to_all(m["kv_cs"], m["kv_c"], group_f)
    start_window(window[2:], False)
    kvg.pop(("kg", 1)).wait_recv()
    forward = [send(m["kg"].at[pl.ds(6, 2)], m["kg"].at[pl.ds(4, 2)], group_j[2])]
    kvg.pop(("vg", 3)).wait_recv()
    forward += [send(m["vg"].at[pl.ds(2, 2)], m["vg"].at[pl.ds(4, 2)], group_j[4])]
    gq = gather(m["q_cs"][...], qcs, m["q_c"])
    start_window(window, True)
    for copy in list(kvg.values()) + forward:
        copy.wait_recv()

    def head_mask(h, width):
        lane_head = lax.broadcasted_iota(jnp.int32, (1, width), 1) // HEAD_DIM
        return jnp.where(lane_head == h, 1.0, 0.0).astype(BF16)

    gq2 = jnp.concatenate([gq * head_mask(0, half), gq * head_mask(1, half)], axis=0)
    peak = None
    for n in range(r):
        s = dot_nt(m["kg"][n].reshape(2 * BLOCK, half), gq2) * LOG2_SCALE
        m["s2"][n] = s
        top = jnp.max(s, axis=0, keepdims=True)
        peak = top if peak is None else jnp.maximum(peak, top)
    total = jnp.zeros((1, 2 * qc), F32)
    acc = jnp.zeros((half, 2 * qc), F32)
    for n in range(r):
        e = jnp.exp2(m["s2"][n] - peak)
        total = total + jnp.sum(e, axis=0, keepdims=True)
        e = e.astype(BF16)
        acc = acc + dot_nn(m["vg"][n, 0], e[:BLOCK]) + dot_nn(m["vg"][n, 1], e[BLOCK:])
    first = lax.broadcasted_iota(jnp.int32, (1, 2 * qc), 1) < qc
    acc = jnp.where(first, acc[:HEAD_DIM], acc[HEAD_DIM:])
    m["o_bs"][...] = (acc / total).astype(BF16)
    m["l_bs"][...] = peak + jnp.log2(total)

    def combine(tag, groups):
        for group in groups:
            group.wait_recv()
        slots = "b" if tag == "bs" else "c"
        size = m["o_" + slots].shape[0]
        logs = [m["l_" + tag][...]] + [m["l_" + slots][n] for n in range(size)]
        peak = functools.reduce(jnp.maximum, logs)
        shares = [jnp.exp2(x - peak) for x in logs]
        total = functools.reduce(jnp.add, shares)
        acc = m["o_" + tag][...].astype(F32) * shares[0]
        for n in range(size):
            acc = acc + m["o_" + slots][n].astype(F32) * shares[n + 1]
        return acc / total, peak + jnp.log2(total)

    ob = [to_all(m["o_bs"], m["o_b"], group_n), to_all(m["l_bs"], m["l_b"], group_n)]

    mine = m["kv_full"].at[part_of(j, ch), part_of(zn, piece)]
    m["kv_full"][part_of(j, ch), part_of(zn, piece)] = gather(m["kv_cs"][...], kvc, m["kv_c"])
    kve = send_all([(mine, mine, dev) for dev in group_n], m["kv_b"])
    partners_next = [
        plan(m[name].at[pl.ds(8 - 8 * c, 2)], m[name].at[pl.ds(6 - 4 * c, 2)], partner)
        for name in ("kx", "vx")
    ]
    beside += partners_next
    inner = (z > 0) & (z < z_n - 1)

    def pass_on():
        for copy in window:
            copy.wait_recv()
        for copy in partners_next:
            copy.start()

    pl.when(inner)(pass_on)

    kve.wait_recv()
    mine = m["kv_full"].at[part_of(j, ch), :]
    kvd = send_all([(mine, mine, dev) for dev in group_j], m["kv_a"])

    o, l = combine("bs", ob)
    m["o_cs"][...] = o.astype(BF16)
    m["l_cs"][...] = l
    oc = [to_all(m["o_cs"], m["o_c"], group_f), to_all(m["l_cs"], m["l_c"], group_f)]

    pl.when(jnp.logical_not(inner))(pass_on)
    loads["rand"].wait()
    for copy in beside:
        copy.wait_recv()
    blocks = 2 * shards

    def queries_of(jb, pair):
        qb_here = m["q"][part_of(jb, BLOCK), :]
        return jnp.concatenate(
            [qb_here * head_mask(2 * pair, FEATS), qb_here * head_mask(2 * pair + 1, FEATS)],
            axis=0,
        )

    def attend_near(step, carry):
        jb = step // 2
        pair = step % 2
        q2 = queries_of(jb, pair)
        feats = part_of(pair, half)
        spots_x = [2 + jb + w for w in range(4)]
        spots_x += [
            jnp.clip(m["rand"][jb, n] - 2 * tm + 2 * SPREAD, 0, 9) for n in range(RAND)
        ]
        peak = None
        for n in range(7):
            s = dot_nt(m["kx"][spots_x[n]], q2) * LOG2_SCALE
            if n in (0, 1, 3):
                block = 2 * tm + jb + n - 2
                inside = (block >= 0) & (block < blocks)
                s = jnp.where(inside, s, NEG)
            m["s"][n] = s
            top = jnp.max(s, axis=0, keepdims=True)
            peak = top if peak is None else jnp.maximum(peak, top)
        total = jnp.zeros((1, 2 * BLOCK), F32)
        acc = jnp.zeros((half, 2 * BLOCK), F32)
        for n in range(7):
            e = jnp.exp2(m["s"][n] - peak)
            total = total + jnp.sum(e, axis=0, keepdims=True)
            acc = acc + dot_nn(m["vx"][spots_x[n], feats, :], e.astype(BF16))
        m["peak"][step] = peak
        m["total"][step] = total
        m["acc"][step] = acc
        return carry

    for step in range(4):
        attend_near(step, 0)

    kvd.wait_recv()
    gv_t = m["kv_full"][:, FEATS:].astype(F32).T.astype(BF16)
    for b in range(2):
        m["gvt"][b] = gv_t[:, b * BLOCK : (b + 1) * BLOCK]

    def attend_global(step, carry):
        jb = step // 2
        pair = step % 2
        q2 = queries_of(jb, pair)
        feats = part_of(pair, half)
        s = dot_nt(m["kv_full"][:, :FEATS], q2) * LOG2_SCALE
        before = m["peak"][step]
        peak = jnp.maximum(before, jnp.max(s, axis=0, keepdims=True))
        e = jnp.exp2(s - peak)
        share = jnp.exp2(before - peak)
        total = m["total"][step] * share + jnp.sum(e, axis=0, keepdims=True)
        e = e.astype(BF16)
        acc = m["acc"][step] * share
        for b in range(2):
            acc = acc + dot_nn(m["gvt"][b, feats, :], e[b * BLOCK : (b + 1) * BLOCK])
        acc = acc / total
        for n in range(2):
            m["att_t"][part_of(pair * 2 + n, HEAD_DIM), part_of(jb, BLOCK)] = acc[
                n * HEAD_DIM : (n + 1) * HEAD_DIM, n * BLOCK : (n + 1) * BLOCK
            ]
        return carry

    for step in range(4):
        attend_global(step, 0)
    is_global = jnp.max(m["pick"][...].astype(F32), axis=1, keepdims=True)
    m["attl"][...] = jnp.where(is_global > 0.5, 0.0, m["att_t"][...].T)

    o, _ = combine("cs", oc)
    o_t = o.T
    o_t = jnp.concatenate([o_t[:qc], o_t[qc:]], axis=1).astype(BF16)
    m["o_full"][part_of(y, qc), part_of(c, half)] = o_t
    mine = m["o_full"].at[part_of(y, qc), part_of(c, half)]
    od = send_all([(mine, mine, dev) for dev in group_j], m["q_a"])
    od.wait_recv()

    placed = dot_nn(m["pick"][...], m["o_full"][...])
    m["att"][...] = (placed + m["attl"][...]).astype(BF16)
    per = TOK // heads
    pieces = [m["att"].at[part_of((hd + d) % heads, per)] for d in range(1, heads)]
    ax = send_all([(src, m["asl"].at[d], group_h[d]) for d, src in enumerate(pieces)], m["asl"])
    mixed = dot_nn(m["att"][part_of(hd, per)], m["osl"][0])
    ow.wait_recv()
    ax.wait_recv()
    for d in range(heads - 1):
        mixed = mixed + dot_nn(m["asl"][d], m["osl"][d + 1])
    out_v[...] = mixed.astype(BF16)
    for copy in started:
        copy.wait_send()


def shards_fn(tokens, q_weight, k_weight, v_weight, o_weight, rand_blocks, global_pos):
    shards = lax.axis_size("tm")
    heads = lax.axis_size("head")
    split = split_of(shards)
    d = tokens.shape[1]
    scratch = scratch_of(split, heads, d)
    hbm = pl.BlockSpec(memory_space=pl.ANY)
    return pl.pallas_call(
        functools.partial(kernel, split, heads, list(scratch)),
        out_shape=jax.ShapeDtypeStruct((TOK // heads, d), BF16),
        in_specs=[hbm] * 7,
        out_specs=pl.BlockSpec(memory_space=pltpu.VMEM),
        scratch_shapes=list(scratch.values()),
        compiler_params=pltpu.CompilerParams(
            collective_id=0, has_side_effects=True, vmem_limit_bytes=VMEM_LIMIT
        ),
        name="layer",
    )(
        tokens,
        q_weight,
        k_weight,
        v_weight,
        o_weight,
        pltpu.with_memory_space_constraint(rand_blocks, pltpu.HBM),
        pltpu.with_memory_space_constraint(global_pos.reshape(1, GLOBALS), pltpu.HBM),
    )


def solution(mesh):
    placed = (
        P("tm", None),
        P(None, "head"),
        P(None, "head"),
        P(None, "head"),
        P("head", None),
        P("tm", None),
        P(),
    )
    return jax.shard_map(
        shards_fn, mesh=mesh, in_specs=placed, out_specs=P(("tm", "head"), None), check_vma=False
    )
```

```python
import functools
import math

import jax
import jax.numpy as jnp
from jax import lax
from jax.experimental import pallas as pl
from jax.experimental.pallas import tpu as pltpu
from jax.sharding import PartitionSpec as P

HEAD_DIM = 64
BLOCK = 128
GLOBALS = 256
RAND = 3
SPREAD = 2
TOK = 256
FEATS = 256
HEADS_HERE = FEATS // HEAD_DIM
LOG2_SCALE = math.log2(math.e) / math.sqrt(HEAD_DIM)
NEG = -1e30
VMEM_LIMIT = 56000000
MESH = pl.DeviceIdType.MESH
F32 = jnp.float32
BF16 = jnp.bfloat16


def dot_nn(a, b):
    return jnp.dot(a, b, preferred_element_type=F32)


def dot_nt(a, b):
    return lax.dot_general(a, b, (((1,), (1,)), ((), ())), preferred_element_type=F32)


def split_of(shards):
    return {128: (4, 4, 4), 32: (4, 2, 2)}[shards]


class Group:
    def __init__(self, going, coming):
        self.wait_send = going.wait
        self.wait_recv = coming.wait


def scratch_of(split, heads, d):
    y_n, zn_n, zf_n = split
    r = 2 * y_n
    qc = GLOBALS // y_n
    piece = qc // zn_n
    vm = pltpu.VMEM
    out = {
        "tok": vm((TOK, d), BF16),
        "wq": vm((d, FEATS), BF16),
        "wk": vm((d, FEATS), BF16),
        "wv": vm((d, FEATS), BF16),
        "osl": vm((heads, FEATS, d), BF16),
        "asl": vm((heads - 1, TOK // heads, FEATS), BF16),
        "att": vm((TOK, FEATS), BF16),
        "attl": vm((TOK, FEATS), F32),
        "att_t": vm((FEATS, TOK), F32),
        "q": vm((TOK, FEATS), BF16),
        "kx": vm((10, BLOCK, FEATS), BF16),
        "vx": vm((10, FEATS, BLOCK), BF16),
        "gvt": vm((2, FEATS, BLOCK), BF16),
        "s": vm((7, BLOCK, 2 * BLOCK), F32),
        "peak": vm((4, 1, 2 * BLOCK), F32),
        "total": vm((4, 1, 2 * BLOCK), F32),
        "acc": vm((4, 2 * HEAD_DIM, 2 * BLOCK), F32),
        "pick": vm((TOK, GLOBALS), BF16),
        "kg": vm((r, 2, BLOCK, 2 * HEAD_DIM), BF16),
        "vg": vm((r, 2, 2 * HEAD_DIM, BLOCK), BF16),
        "s2": vm((r, 2 * BLOCK, 2 * qc), F32),
        "q_part": vm((GLOBALS, FEATS), BF16),
        "q_a": vm((r - 1, qc, 2 * HEAD_DIM), BF16),
        "q_bs": vm((qc, 2 * HEAD_DIM), BF16),
        "q_b": vm((zn_n - 1, qc, 2 * HEAD_DIM), BF16),
        "q_cs": vm((qc, 2 * HEAD_DIM), BF16),
        "q_c": vm((zf_n - 1, qc, 2 * HEAD_DIM), BF16),
        "kv_part": vm((GLOBALS, 2 * FEATS), BF16),
        "kv_p": vm((GLOBALS, FEATS), BF16),
        "kv_ps": vm((GLOBALS, FEATS), BF16),
        "kv_a": vm((y_n - 1, qc, FEATS), BF16),
        "kv_bs": vm((qc, FEATS), BF16),
        "kv_b": vm((zn_n - 1, piece, FEATS), BF16),
        "kv_cs": vm((piece, FEATS), BF16),
        "kv_c": vm((zf_n - 1, piece, FEATS), BF16),
        "kv_size": vm((r - 1, qc, FEATS), BF16),
        "kv_full": vm((GLOBALS, 2 * FEATS), BF16),
        "o_bs": vm((HEAD_DIM, 2 * qc), BF16),
        "o_b": vm((zn_n - 1, HEAD_DIM, 2 * qc), BF16),
        "o_cs": vm((HEAD_DIM, 2 * qc), BF16),
        "o_c": vm((zf_n - 1, HEAD_DIM, 2 * qc), BF16),
        "o_full": vm((GLOBALS, FEATS), BF16),
        "l_bs": vm((1, 2 * qc), F32),
        "l_b": vm((zn_n - 1, 1, 2 * qc), F32),
        "l_cs": vm((1, 2 * qc), F32),
        "l_c": vm((zf_n - 1, 1, 2 * qc), F32),
        "grow": vm((1, GLOBALS), jnp.int32),
        "rand": pltpu.SMEM((2, RAND), jnp.int32),
    }
    copies = 31 + heads - 1
    out["send"] = pltpu.SemaphoreType.DMA((copies,))
    out["recv"] = pltpu.SemaphoreType.DMA((copies,))
    out["greet"] = pltpu.SemaphoreType.REGULAR
    out["load"] = pltpu.SemaphoreType.DMA((7,))
    return out


def kernel(split, heads, names, tok_h, wq_h, wk_h, wv_h, ow_h, rand_h, grow_h, out_v, *scratch):
    m = dict(zip(names, scratch))
    y_n, zn_n, zf_n = split
    r = 2 * y_n
    qc = GLOBALS // y_n
    piece = qc // zn_n
    half = 2 * HEAD_DIM
    shards = r * zn_n * zf_n
    z_n = zn_n * zf_n
    tm = lax.axis_index("tm")
    hd = lax.axis_index("head")

    order = (("tok", tok_h), ("wq", wq_h), ("grow", grow_h), ("wk", wk_h), ("wv", wv_h))
    order += (("osl", ow_h), ("rand", rand_h))
    loads = {}
    for i, (name, src) in enumerate(order):
        dst = m[name].at[0] if name == "osl" else m[name]
        loads[name] = pltpu.make_async_copy(src, dst, m["load"].at[i])
    for name in ("tok", "wq", "grow"):
        loads[name].start()

    y = tm // (2 * z_n)
    z = (tm // 2) % z_n
    c = tm % 2
    j = y * 2 + c
    zn = z % zn_n
    zf = z // zn_n

    def dev_yc(yy, cc):
        return (yy * (2 * z_n) + z * 2 + cc, hd)

    def dev_z(zz):
        return (y * (2 * z_n) + zz * 2 + c, hd)

    steps_j = [(2, 0), (2, 1), (1, 0), (1, 1), (3, 0), (3, 1), (0, 1)]
    there = [((y + dy) % y_n, (c + e) % 2) for dy, e in steps_j]
    group_j = [dev_yc(*at) for at in there]
    near = [(zn + d) % zn_n for d in range(1, zn_n)]
    group_n = [dev_z(zf * zn_n + at) for at in near]
    far_steps = sorted(range(1, zf_n), key=lambda d: -min(d, zf_n - d))
    group_f = [dev_z(((zf + d) % zf_n) * zn_n + zn) for d in far_steps]
    group_h = [(tm, (hd + d) % heads) for d in range(1, heads)]
    steps_w = (2, -2)
    partner = dev_yc(y, 1 - c)
    group_w = [((tm + d + shards) % shards, hd) for d in steps_w]
    next_f = [dev for d, dev in zip(far_steps, group_f) if min(d, zf_n - d) == 1]
    relayed = len(next_f) < len(group_f)
    everyone = next_f + group_n + group_w + group_j + group_h

    barrier = pltpu.get_barrier_semaphore()
    for dev in everyone:
        pl.semaphore_signal(barrier, inc=1, device_id=dev, device_id_type=MESH)
    for name in ("wk", "wv", "osl", "rand"):
        loads[name].start()

    count = [0]
    started = []

    def plan(src, dst, dev):
        n = count[0]
        count[0] += 1
        copy = pltpu.make_async_remote_copy(
            src_ref=src,
            dst_ref=dst,
            send_sem=m["send"].at[n],
            recv_sem=m["recv"].at[n],
            device_id=dev,
            device_id_type=MESH,
        )
        started.append(copy)
        return copy

    def send(src, dst, dev):
        copy = plan(src, dst, dev)
        copy.start()
        return copy

    def send_all(items, like):
        n = count[0]
        count[0] += 1
        for src, dst, dev in items:
            pltpu.make_async_remote_copy(
                src_ref=src,
                dst_ref=dst,
                send_sem=m["send"].at[n],
                recv_sem=m["recv"].at[n],
                device_id=dev,
                device_id_type=MESH,
            ).start()
        group = Group(*(pltpu.make_async_copy(like, like, m[way].at[n]) for way in ("send", "recv")))
        started.append(group)
        return group

    def part_of(at, size):
        return pl.ds(pl.multiple_of(at * size, size), size)

    def gather(first, group, slots):
        group.wait_recv()
        total = first.astype(F32)
        for n in range(slots.shape[0]):
            total = total + slots[n].astype(F32)
        return total.astype(BF16)

    def to_all(src, dst, group):
        return send_all([(src, dst.at[n], dev) for n, dev in enumerate(group)], dst)

    loads["grow"].wait()
    spots = lax.broadcasted_iota(jnp.int32, (TOK, GLOBALS), 0) + tm * TOK
    pick = jnp.where(spots == m["grow"][...], 1.0, 0.0).astype(F32)
    m["pick"][...] = pick.astype(BF16)
    pick_t = pick.T.astype(BF16)
    loads["tok"].wait()
    loads["wq"].wait()
    q = dot_nn(m["tok"][...], m["wq"][...]).astype(BF16)
    m["q"][...] = q
    m["q_part"][...] = dot_nn(pick_t, q).astype(BF16)
    pl.semaphore_wait(barrier, len(everyone))
    if relayed:
        for dev in next_f:
            pl.semaphore_signal(m["greet"], inc=1, device_id=dev, device_id_type=MESH)
    pieces = [m["q_part"].at[part_of(yy, qc), part_of(cc, half)] for yy, cc in there]
    qa = send_all([(src, m["q_a"].at[n], group_j[n]) for n, src in enumerate(pieces)], m["q_a"])

    loads["wk"].wait()
    k = dot_nn(m["tok"][...], m["wk"][...]).astype(BF16)
    m["kv_part"][:, :FEATS] = dot_nn(pick_t, k).astype(BF16)
    for b in range(2):
        m["kx"][4 + b] = k[b * BLOCK : (b + 1) * BLOCK]
    loads["wv"].wait()
    v32 = dot_nn(m["tok"][...], m["wv"][...])
    m["kv_part"][:, FEATS:] = dot_nn(pick_t, v32.astype(BF16)).astype(BF16)
    kvp = send(m["kv_part"].at[:, part_of(1 - c, FEATS)], m["kv_p"], partner)
    v_t = v32.T.astype(BF16)
    for b in range(2):
        m["vx"][4 + b] = v_t[:, b * BLOCK : (b + 1) * BLOCK]


    edges = (z == z_n - 1, z == 0)
    window, beside = [], []
    for name in ("kx", "vx"):
        own = m[name].at[pl.ds(4, 2)]
        for step, dev in zip(steps_w, group_w):
            window.append(plan(own, m[name].at[pl.ds(2 * (SPREAD - step), 2)], dev))
        beside.append(send(own, m[name].at[pl.ds(2 + 4 * c, 2)], partner))

    def start_window(copies, at_edge):
        for n, copy in enumerate(copies):
            pl.when(edges[n % 2] if at_edge else jnp.logical_not(edges[n % 2]))(copy.start)

    start_window(window[:2], False)
    loads["osl"].wait()
    ow = send_all(
        [(m["osl"].at[0], m["osl"].at[d + 1], dev) for d, dev in enumerate(group_h)],
        m["osl"].at[pl.ds(1, heads - 1)],
    )
    for b in range(2):
        m["kg"][0, b] = m["kx"][4 + b, :, part_of(c, half)]
        m["vg"][0, b] = m["vx"][4 + b, part_of(c, half), :]

    kvp.wait_recv()
    m["kv_ps"][...] = (
        m["kv_part"][:, part_of(c, FEATS)].astype(F32) + m["kv_p"][...].astype(F32)
    ).astype(BF16)
    same = [n for n, step in enumerate(steps_j) if step[1] == 0]
    kva = send_all(
        [
            (m["kv_ps"].at[part_of(there[n][0], qc)], m["kv_a"].at[i], group_j[n])
            for i, n in enumerate(same)
        ],
        m["kv_a"],
    )
    m["q_bs"][...] = gather(m["q_part"][part_of(y, qc), part_of(c, half)], qa, m["q_a"])
    qb = to_all(m["q_bs"], m["q_b"], group_n)
    kvg = {}
    for dy in (1, 3, 0):
        at = [n for n, step in enumerate(steps_j) if step[0] == dy]
        slots = [((y_n - dy) % y_n) * 2 + steps_j[n][1] for n in at]
        ways = [(m["kx"].at[pl.ds(4, 2), :, part_of(there[n][1], half)], "kg") for n in at]
        ways = [ways] + [
            [(m["vx"].at[pl.ds(4, 2), part_of(there[n][1], half), :], "vg") for n in at]
        ]
        for way in ways if dy == 1 else ways[::-1]:
            name = way[0][1]
            kvg[(name, dy)] = send_all(
                [(way[i][0], m[name].at[slots[i]], group_j[n]) for i, n in enumerate(at)],
                m[name].at[pl.ds(0, len(at))],
            )
    m["kv_bs"][...] = gather(m["kv_ps"][part_of(y, qc), :], kva, m["kv_a"])
    pieces = [m["kv_bs"].at[part_of(at, piece)] for at in near]
    kvb = send_all([(src, m["kv_b"].at[n], group_n[n]) for n, src in enumerate(pieces)], m["kv_b"])
    m["q_cs"][...] = gather(m["q_bs"][...], qb, m["q_b"])
    if relayed:
        pl.semaphore_wait(m["greet"], len(next_f))
    qcs = to_all(m["q_cs"], m["q_c"], group_f)
    kvg.pop(("kg", 1)).wait_recv()
    forward = [send(m["kg"].at[pl.ds(6, 2)], m["kg"].at[pl.ds(4, 2)], group_j[2])]
    kvg.pop(("vg", 3)).wait_recv()
    forward += [send(m["vg"].at[pl.ds(2, 2)], m["vg"].at[pl.ds(4, 2)], group_j[4])]

    m["kv_cs"][...] = gather(m["kv_bs"][part_of(zn, piece), :], kvb, m["kv_b"])
    kvc = to_all(m["kv_cs"], m["kv_c"], group_f)
    start_window(window[2:], False)
    gq = gather(m["q_cs"][...], qcs, m["q_c"])
    start_window(window, True)
    for copy in list(kvg.values()) + forward:
        copy.wait_recv()

    def head_mask(h, width):
        lane_head = lax.broadcasted_iota(jnp.int32, (1, width), 1) // HEAD_DIM
        return jnp.where(lane_head == h, 1.0, 0.0).astype(BF16)

    gq2 = jnp.concatenate([gq * head_mask(0, half), gq * head_mask(1, half)], axis=0)
    peak = None
    for n in range(r):
        s = dot_nt(m["kg"][n].reshape(2 * BLOCK, half), gq2) * LOG2_SCALE
        m["s2"][n] = s
        top = jnp.max(s, axis=0, keepdims=True)
        peak = top if peak is None else jnp.maximum(peak, top)
    total = jnp.zeros((1, 2 * qc), F32)
    acc = jnp.zeros((half, 2 * qc), F32)
    for n in range(r):
        e = jnp.exp2(m["s2"][n] - peak)
        total = total + jnp.sum(e, axis=0, keepdims=True)
        e = e.astype(BF16)
        acc = acc + dot_nn(m["vg"][n, 0], e[:BLOCK]) + dot_nn(m["vg"][n, 1], e[BLOCK:])
    first = lax.broadcasted_iota(jnp.int32, (1, 2 * qc), 1) < qc
    acc = jnp.where(first, acc[:HEAD_DIM], acc[HEAD_DIM:])
    m["o_bs"][...] = (acc / total).astype(BF16)
    m["l_bs"][...] = peak + jnp.log2(total)

    def combine(tag, groups):
        for group in groups:
            group.wait_recv()
        slots = "b" if tag == "bs" else "c"
        size = m["o_" + slots].shape[0]
        logs = [m["l_" + tag][...]] + [m["l_" + slots][n] for n in range(size)]
        peak = functools.reduce(jnp.maximum, logs)
        shares = [jnp.exp2(x - peak) for x in logs]
        total = functools.reduce(jnp.add, shares)
        acc = m["o_" + tag][...].astype(F32) * shares[0]
        for n in range(size):
            acc = acc + m["o_" + slots][n].astype(F32) * shares[n + 1]
        return acc / total, peak + jnp.log2(total)

    ob = [to_all(m["o_bs"], m["o_b"], group_n), to_all(m["l_bs"], m["l_b"], group_n)]

    mine = m["kv_full"].at[part_of(y * zn_n + zn, piece), part_of(c, FEATS)]
    m["kv_full"][part_of(y * zn_n + zn, piece), part_of(c, FEATS)] = gather(m["kv_cs"][...], kvc, m["kv_c"])
    kve = send_all([(mine, mine, dev) for dev in group_n], m["kv_b"])
    partners_next = [
        plan(m[name].at[pl.ds(8 - 8 * c, 2)], m[name].at[pl.ds(6 - 4 * c, 2)], partner)
        for name in ("kx", "vx")
    ]
    beside += partners_next
    inner = (z > 0) & (z < z_n - 1)

    def pass_on():
        for n, copy in enumerate(partners_next):
            for arriving in window[2 * n : 2 * n + 2]:
                arriving.wait_recv()
            copy.start()

    pl.when(inner)(pass_on)

    o, l = combine("bs", ob)
    m["o_cs"][...] = o.astype(BF16)
    m["l_cs"][...] = l
    oc = [to_all(m["o_cs"], m["o_c"], group_f), to_all(m["l_cs"], m["l_c"], group_f)]

    kve.wait_recv()
    mine = m["kv_full"].at[part_of(y, qc), part_of(c, FEATS)]
    kvd = send_all([(mine, mine, dev) for dev in group_j], m["kv_size"])
    pl.when(jnp.logical_not(inner))(pass_on)
    loads["rand"].wait()
    for copy in beside:
        copy.wait_recv()
    blocks = 2 * shards

    def queries_of(jb, pair):
        qb_here = m["q"][part_of(jb, BLOCK), :]
        return jnp.concatenate(
            [qb_here * head_mask(2 * pair, FEATS), qb_here * head_mask(2 * pair + 1, FEATS)],
            axis=0,
        )

    def attend_near(step, carry):
        jb = step // 2
        pair = step % 2
        q2 = queries_of(jb, pair)
        feats = part_of(pair, half)
        spots_x = [2 + jb + w for w in range(4)]
        spots_x += [
            jnp.clip(m["rand"][jb, n] - 2 * tm + 2 * SPREAD, 0, 9) for n in range(RAND)
        ]
        peak = None
        for n in range(7):
            s = dot_nt(m["kx"][spots_x[n]], q2) * LOG2_SCALE
            if n in (0, 1, 3):
                block = 2 * tm + jb + n - 2
                inside = (block >= 0) & (block < blocks)
                s = jnp.where(inside, s, NEG)
            m["s"][n] = s
            top = jnp.max(s, axis=0, keepdims=True)
            peak = top if peak is None else jnp.maximum(peak, top)
        total = jnp.zeros((1, 2 * BLOCK), F32)
        acc = jnp.zeros((half, 2 * BLOCK), F32)
        for at in ((0, 1), (2, 3), (4, 5), (6,)):
            weights, values = [], []
            for n in at:
                e = jnp.exp2(m["s"][n] - peak)
                total = total + jnp.sum(e, axis=0, keepdims=True)
                weights.append(e.astype(BF16))
                values.append(m["vx"][spots_x[n], feats, :])
            acc = acc + dot_nn(jnp.concatenate(values, axis=1), jnp.concatenate(weights, axis=0))
        m["peak"][step] = peak
        m["total"][step] = total
        m["acc"][step] = acc
        return carry

    for step in range(4):
        attend_near(step, 0)

    kvd.wait_recv()
    gv_t = m["kv_full"][:, FEATS:].astype(F32).T.astype(BF16)
    for b in range(2):
        m["gvt"][b] = gv_t[:, b * BLOCK : (b + 1) * BLOCK]

    def attend_global(step, carry):
        jb = step // 2
        pair = step % 2
        q2 = queries_of(jb, pair)
        feats = part_of(pair, half)
        s = dot_nt(m["kv_full"][:, :FEATS], q2) * LOG2_SCALE
        before = m["peak"][step]
        peak = jnp.maximum(before, jnp.max(s, axis=0, keepdims=True))
        e = jnp.exp2(s - peak)
        share = jnp.exp2(before - peak)
        total = m["total"][step] * share + jnp.sum(e, axis=0, keepdims=True)
        e = e.astype(BF16)
        acc = m["acc"][step] * share
        acc = acc + dot_nn(jnp.concatenate([m["gvt"][b, feats, :] for b in range(2)], axis=1), e)
        acc = acc / total
        for n in range(2):
            m["att_t"][part_of(pair * 2 + n, HEAD_DIM), part_of(jb, BLOCK)] = acc[
                n * HEAD_DIM : (n + 1) * HEAD_DIM, n * BLOCK : (n + 1) * BLOCK
            ]
        return carry

    for step in range(4):
        attend_global(step, 0)
    is_global = jnp.max(m["pick"][...].astype(F32), axis=1, keepdims=True)
    m["attl"][...] = jnp.where(is_global > 0.5, 0.0, m["att_t"][...].T)

    o, _ = combine("cs", oc)
    o_t = o.T
    o_t = jnp.concatenate([o_t[:qc], o_t[qc:]], axis=1).astype(BF16)
    m["o_full"][part_of(y, qc), part_of(c, half)] = o_t
    mine = m["o_full"].at[part_of(y, qc), part_of(c, half)]
    od = send_all([(mine, mine, dev) for dev in group_j], m["q_a"])
    od.wait_recv()

    placed = dot_nn(m["pick"][...], m["o_full"][...])
    m["att"][...] = (placed + m["attl"][...]).astype(BF16)
    per = TOK // heads
    x_steps = sorted(range(1, heads), key=lambda d: -min(d, heads - d))
    ax = {
        d: send(m["att"].at[part_of((hd + d) % heads, per)], m["asl"].at[d - 1], group_h[d - 1])
        for d in x_steps
    }
    mixed = dot_nn(m["att"][part_of(hd, per)], m["osl"][0])
    ow.wait_recv()
    for d in x_steps[::-1]:
        ax[d].wait_recv()
        mixed = mixed + dot_nn(m["asl"][d - 1], m["osl"][d])
    out_v[...] = mixed.astype(BF16)
    for copy in started:
        copy.wait_send()


def shards_fn(tokens, q_weight, k_weight, v_weight, o_weight, rand_blocks, global_pos):
    shards = lax.axis_size("tm")
    heads = lax.axis_size("head")
    split = split_of(shards)
    d = tokens.shape[1]
    scratch = scratch_of(split, heads, d)
    hbm = pl.BlockSpec(memory_space=pl.ANY)
    return pl.pallas_call(
        functools.partial(kernel, split, heads, list(scratch)),
        out_shape=jax.ShapeDtypeStruct((TOK // heads, d), BF16),
        in_specs=[hbm] * 7,
        out_specs=pl.BlockSpec(memory_space=pltpu.VMEM),
        scratch_shapes=list(scratch.values()),
        compiler_params=pltpu.CompilerParams(
            collective_id=0, has_side_effects=True, vmem_limit_bytes=VMEM_LIMIT
        ),
        name="layer",
    )(
        tokens,
        q_weight,
        k_weight,
        v_weight,
        o_weight,
        pltpu.with_memory_space_constraint(rand_blocks, pltpu.HBM),
        pltpu.with_memory_space_constraint(global_pos.reshape(1, GLOBALS), pltpu.HBM),
    )


def solution(mesh):
    placed = (
        P("tm", None),
        P(None, "head"),
        P(None, "head"),
        P(None, "head"),
        P("head", None),
        P("tm", None),
        P(),
    )
    return jax.shard_map(
        shards_fn, mesh=mesh, in_specs=placed, out_specs=P(("tm", "head"), None), check_vma=False
    )
```

```python
import functools
import math

import jax
import jax.numpy as jnp
from jax import lax
from jax.experimental import pallas as pl
from jax.experimental.pallas import tpu as pltpu
from jax.sharding import PartitionSpec as P

HEAD_DIM = 64
BLOCK = 128
GLOBALS = 256
RAND = 3
SPREAD = 2
TOK = 256
FEATS = 256
HEADS_HERE = FEATS // HEAD_DIM
LOG2_SCALE = math.log2(math.e) / math.sqrt(HEAD_DIM)
NEG = -1e30
VMEM_LIMIT = 56000000
MESH = pl.DeviceIdType.MESH
F32 = jnp.float32
BF16 = jnp.bfloat16


def dot_nn(a, b):
    return jnp.dot(a, b, preferred_element_type=F32)


def dot_nt(a, b):
    return lax.dot_general(a, b, (((1,), (1,)), ((), ())), preferred_element_type=F32)


def split_of(shards):
    return {128: (4, 4, 4), 32: (4, 2, 2)}[shards]


class Group:
    def __init__(self, going, coming):
        self.wait_send = going.wait
        self.wait_recv = coming.wait


def scratch_of(split, heads, d):
    y_n, zn_n, zf_n = split
    r = 2 * y_n
    qc = GLOBALS // y_n
    piece = qc // zn_n
    vm = pltpu.VMEM
    out = {
        "tok": vm((TOK, d), BF16),
        "wq": vm((d, FEATS), BF16),
        "wk": vm((d, FEATS), BF16),
        "wv": vm((d, FEATS), BF16),
        "osl": vm((heads, FEATS, d), BF16),
        "asl": vm((heads - 1, TOK // heads, FEATS), BF16),
        "att": vm((TOK, FEATS), BF16),
        "attl": vm((TOK, FEATS), F32),
        "att_t": vm((FEATS, TOK), F32),
        "q": vm((TOK, FEATS), BF16),
        "kx": vm((10, BLOCK, FEATS), BF16),
        "vx": vm((10, FEATS, BLOCK), BF16),
        "gvt": vm((2, FEATS, BLOCK), BF16),
        "s": vm((7, BLOCK, 2 * BLOCK), F32),
        "peak": vm((4, 1, 2 * BLOCK), F32),
        "total": vm((4, 1, 2 * BLOCK), F32),
        "acc": vm((4, 2 * HEAD_DIM, 2 * BLOCK), F32),
        "pick": vm((TOK, GLOBALS), BF16),
        "kg": vm((r, 2, BLOCK, 2 * HEAD_DIM), BF16),
        "vg": vm((r, 2, 2 * HEAD_DIM, BLOCK), BF16),
        "s2": vm((r, 2 * BLOCK, 2 * qc), F32),
        "q_part": vm((GLOBALS, FEATS), BF16),
        "q_a": vm((r - 1, qc, 2 * HEAD_DIM), BF16),
        "q_bs": vm((qc, 2 * HEAD_DIM), BF16),
        "q_b": vm((zn_n - 1, qc, 2 * HEAD_DIM), BF16),
        "q_cs": vm((qc, 2 * HEAD_DIM), BF16),
        "q_c": vm((zf_n - 1, qc, 2 * HEAD_DIM), BF16),
        "kv_part": vm((GLOBALS, 2 * FEATS), BF16),
        "kv_p": vm((GLOBALS, FEATS), BF16),
        "kv_ps": vm((GLOBALS, FEATS), BF16),
        "kv_a": vm((y_n - 1, qc, FEATS), BF16),
        "kv_bs": vm((qc, FEATS), BF16),
        "kv_b": vm((zn_n - 1, piece, FEATS), BF16),
        "kv_cs": vm((piece, FEATS), BF16),
        "kv_c": vm((zf_n - 1, piece, FEATS), BF16),
        "kv_size": vm((r - 1, qc, FEATS), BF16),
        "kv_full": vm((GLOBALS, 2 * FEATS), BF16),
        "o_bs": vm((HEAD_DIM, 2 * qc), BF16),
        "o_b": vm((zn_n - 1, HEAD_DIM, 2 * qc), BF16),
        "o_cs": vm((HEAD_DIM, 2 * qc), BF16),
        "o_c": vm((zf_n - 1, HEAD_DIM, 2 * qc), BF16),
        "o_full": vm((GLOBALS, FEATS), BF16),
        "l_bs": vm((1, 2 * qc), F32),
        "l_b": vm((zn_n - 1, 1, 2 * qc), F32),
        "l_cs": vm((1, 2 * qc), F32),
        "l_c": vm((zf_n - 1, 1, 2 * qc), F32),
        "grow": vm((1, GLOBALS), jnp.int32),
        "rand": pltpu.SMEM((2, RAND), jnp.int32),
    }
    copies = 31 + heads - 1
    out["send"] = pltpu.SemaphoreType.DMA((copies,))
    out["recv"] = pltpu.SemaphoreType.DMA((copies,))
    out["greet"] = pltpu.SemaphoreType.REGULAR
    out["load"] = pltpu.SemaphoreType.DMA((7,))
    return out


def kernel(split, heads, names, tok_h, wq_h, wk_h, wv_h, ow_h, rand_h, grow_h, out_v, *scratch):
    m = dict(zip(names, scratch))
    y_n, zn_n, zf_n = split
    r = 2 * y_n
    qc = GLOBALS // y_n
    piece = qc // zn_n
    half = 2 * HEAD_DIM
    shards = r * zn_n * zf_n
    z_n = zn_n * zf_n
    tm = lax.axis_index("tm")
    hd = lax.axis_index("head")

    order = (("tok", tok_h), ("wq", wq_h), ("grow", grow_h), ("wk", wk_h), ("wv", wv_h))
    order += (("osl", ow_h), ("rand", rand_h))
    loads = {}
    for i, (name, src) in enumerate(order):
        dst = m[name].at[0] if name == "osl" else m[name]
        loads[name] = pltpu.make_async_copy(src, dst, m["load"].at[i])
    for name in ("tok", "wq", "grow"):
        loads[name].start()

    y = tm // (2 * z_n)
    z = (tm // 2) % z_n
    c = tm % 2
    j = y * 2 + c
    zn = z % zn_n
    zf = z // zn_n

    def dev_yc(yy, cc):
        return (yy * (2 * z_n) + z * 2 + cc, hd)

    def dev_z(zz):
        return (y * (2 * z_n) + zz * 2 + c, hd)

    steps_j = [(2, 0), (2, 1), (1, 0), (1, 1), (3, 0), (3, 1), (0, 1)]
    there = [((y + dy) % y_n, (c + e) % 2) for dy, e in steps_j]
    group_j = [dev_yc(*at) for at in there]
    near = [(zn + d) % zn_n for d in range(1, zn_n)]
    group_n = [dev_z(zf * zn_n + at) for at in near]
    far_steps = sorted(range(1, zf_n), key=lambda d: -min(d, zf_n - d))
    group_f = [dev_z(((zf + d) % zf_n) * zn_n + zn) for d in far_steps]
    group_h = [(tm, (hd + d) % heads) for d in range(1, heads)]
    steps_w = (2, -2)
    partner = dev_yc(y, 1 - c)
    group_w = [((tm + d + shards) % shards, hd) for d in steps_w]
    next_f = [dev for d, dev in zip(far_steps, group_f) if min(d, zf_n - d) == 1]
    relayed = len(next_f) < len(group_f)
    everyone = next_f + group_n + group_w + group_j + group_h

    barrier = pltpu.get_barrier_semaphore()
    for dev in everyone:
        pl.semaphore_signal(barrier, inc=1, device_id=dev, device_id_type=MESH)
    for name in ("wk", "wv", "osl", "rand"):
        loads[name].start()

    count = [0]
    started = []

    def plan(src, dst, dev):
        n = count[0]
        count[0] += 1
        copy = pltpu.make_async_remote_copy(
            src_ref=src,
            dst_ref=dst,
            send_sem=m["send"].at[n],
            recv_sem=m["recv"].at[n],
            device_id=dev,
            device_id_type=MESH,
        )
        started.append(copy)
        return copy

    def send(src, dst, dev):
        copy = plan(src, dst, dev)
        copy.start()
        return copy

    def send_all(items, like):
        n = count[0]
        count[0] += 1
        for src, dst, dev in items:
            pltpu.make_async_remote_copy(
                src_ref=src,
                dst_ref=dst,
                send_sem=m["send"].at[n],
                recv_sem=m["recv"].at[n],
                device_id=dev,
                device_id_type=MESH,
            ).start()
        group = Group(*(pltpu.make_async_copy(like, like, m[way].at[n]) for way in ("send", "recv")))
        started.append(group)
        return group

    def part_of(at, size):
        return pl.ds(pl.multiple_of(at * size, size), size)

    def gather(first, group, slots):
        group.wait_recv()
        total = first.astype(F32)
        for n in range(slots.shape[0]):
            total = total + slots[n].astype(F32)
        return total.astype(BF16)

    def to_all(src, dst, group):
        return send_all([(src, dst.at[n], dev) for n, dev in enumerate(group)], dst)

    loads["grow"].wait()
    spots = lax.broadcasted_iota(jnp.int32, (TOK, GLOBALS), 0) + tm * TOK
    pick = jnp.where(spots == m["grow"][...], 1.0, 0.0).astype(F32)
    m["pick"][...] = pick.astype(BF16)
    pick_t = pick.T.astype(BF16)
    loads["tok"].wait()
    loads["wq"].wait()
    q = dot_nn(m["tok"][...], m["wq"][...]).astype(BF16)
    m["q"][...] = q
    m["q_part"][...] = dot_nn(pick_t, q).astype(BF16)
    pl.semaphore_wait(barrier, len(everyone))
    if relayed:
        for dev in next_f:
            pl.semaphore_signal(m["greet"], inc=1, device_id=dev, device_id_type=MESH)
    pieces = [m["q_part"].at[part_of(yy, qc), part_of(cc, half)] for yy, cc in there]
    qa = send_all([(src, m["q_a"].at[n], group_j[n]) for n, src in enumerate(pieces)], m["q_a"])

    loads["wk"].wait()
    k = dot_nn(m["tok"][...], m["wk"][...]).astype(BF16)
    m["kv_part"][:, :FEATS] = dot_nn(pick_t, k).astype(BF16)
    for b in range(2):
        m["kx"][4 + b] = k[b * BLOCK : (b + 1) * BLOCK]
    loads["wv"].wait()
    v32 = dot_nn(m["tok"][...], m["wv"][...])
    m["kv_part"][:, FEATS:] = dot_nn(pick_t, v32.astype(BF16)).astype(BF16)
    kvp = send(m["kv_part"].at[:, part_of(1 - c, FEATS)], m["kv_p"], partner)
    v_t = v32.T.astype(BF16)
    for b in range(2):
        m["vx"][4 + b] = v_t[:, b * BLOCK : (b + 1) * BLOCK]


    edges = (z == z_n - 1, z == 0)
    window, beside = [], []
    for name in ("kx", "vx"):
        own = m[name].at[pl.ds(4, 2)]
        for step, dev in zip(steps_w, group_w):
            window.append(plan(own, m[name].at[pl.ds(2 * (SPREAD - step), 2)], dev))
        beside.append(send(own, m[name].at[pl.ds(2 + 4 * c, 2)], partner))

    def start_window(copies):
        for n, copy in enumerate(copies):
            pl.when(jnp.logical_not(edges[n % 2]))(copy.start)

    def start_edge(ahead):
        for n, copy in enumerate(window):
            first = c == (n + 1) % 2
            turn = first if ahead else jnp.logical_not(first)
            pl.when(edges[n % 2] & turn)(copy.start)

    start_window(window[:2])
    loads["osl"].wait()
    ow = send_all(
        [(m["osl"].at[0], m["osl"].at[d + 1], dev) for d, dev in enumerate(group_h)],
        m["osl"].at[pl.ds(1, heads - 1)],
    )
    for b in range(2):
        m["kg"][0, b] = m["kx"][4 + b, :, part_of(c, half)]
        m["vg"][0, b] = m["vx"][4 + b, part_of(c, half), :]

    kvp.wait_recv()
    m["kv_ps"][...] = (
        m["kv_part"][:, part_of(c, FEATS)].astype(F32) + m["kv_p"][...].astype(F32)
    ).astype(BF16)
    same = [n for n, step in enumerate(steps_j) if step[1] == 0]
    kva = send_all(
        [
            (m["kv_ps"].at[part_of(there[n][0], qc)], m["kv_a"].at[i], group_j[n])
            for i, n in enumerate(same)
        ],
        m["kv_a"],
    )
    m["q_bs"][...] = gather(m["q_part"][part_of(y, qc), part_of(c, half)], qa, m["q_a"])
    qb = to_all(m["q_bs"], m["q_b"], group_n)
    kvg = {}
    for dy in (1, 3, 0):
        at = [n for n, step in enumerate(steps_j) if step[0] == dy]
        slots = [((y_n - dy) % y_n) * 2 + steps_j[n][1] for n in at]
        ways = [(m["kx"].at[pl.ds(4, 2), :, part_of(there[n][1], half)], "kg") for n in at]
        ways = [ways] + [
            [(m["vx"].at[pl.ds(4, 2), part_of(there[n][1], half), :], "vg") for n in at]
        ]
        for way in ways if dy == 1 else ways[::-1]:
            name = way[0][1]
            kvg[(name, dy)] = send_all(
                [(way[i][0], m[name].at[slots[i]], group_j[n]) for i, n in enumerate(at)],
                m[name].at[pl.ds(0, len(at))],
            )
    m["kv_bs"][...] = gather(m["kv_ps"][part_of(y, qc), :], kva, m["kv_a"])
    pieces = [m["kv_bs"].at[part_of(at, piece)] for at in near]
    kvb = send_all([(src, m["kv_b"].at[n], group_n[n]) for n, src in enumerate(pieces)], m["kv_b"])
    m["q_cs"][...] = gather(m["q_bs"][...], qb, m["q_b"])
    if relayed:
        pl.semaphore_wait(m["greet"], len(next_f))
    qcs = to_all(m["q_cs"], m["q_c"], group_f)
    kvg.pop(("kg", 1)).wait_recv()
    forward = [send(m["kg"].at[pl.ds(6, 2)], m["kg"].at[pl.ds(4, 2)], group_j[2])]
    kvg.pop(("vg", 3)).wait_recv()
    forward += [send(m["vg"].at[pl.ds(2, 2)], m["vg"].at[pl.ds(4, 2)], group_j[4])]

    m["kv_cs"][...] = gather(m["kv_bs"][part_of(zn, piece), :], kvb, m["kv_b"])
    kvc = to_all(m["kv_cs"], m["kv_c"], group_f)
    start_window(window[2:])
    gq = gather(m["q_cs"][...], qcs, m["q_c"])
    start_edge(True)
    for copy in list(kvg.values()) + forward:
        copy.wait_recv()
    start_edge(False)

    def head_mask(h, width):
        lane_head = lax.broadcasted_iota(jnp.int32, (1, width), 1) // HEAD_DIM
        return jnp.where(lane_head == h, 1.0, 0.0).astype(BF16)

    gq2 = jnp.concatenate([gq * head_mask(0, half), gq * head_mask(1, half)], axis=0)
    peak = None
    for n in range(r):
        s = dot_nt(m["kg"][n].reshape(2 * BLOCK, half), gq2) * LOG2_SCALE
        m["s2"][n] = s
        top = jnp.max(s, axis=0, keepdims=True)
        peak = top if peak is None else jnp.maximum(peak, top)
    total = jnp.zeros((1, 2 * qc), F32)
    acc = jnp.zeros((half, 2 * qc), F32)
    for n in range(r):
        e = jnp.exp2(m["s2"][n] - peak)
        total = total + jnp.sum(e, axis=0, keepdims=True)
        e = e.astype(BF16)
        acc = acc + dot_nn(m["vg"][n, 0], e[:BLOCK]) + dot_nn(m["vg"][n, 1], e[BLOCK:])
    first = lax.broadcasted_iota(jnp.int32, (1, 2 * qc), 1) < qc
    acc = jnp.where(first, acc[:HEAD_DIM], acc[HEAD_DIM:])
    m["o_bs"][...] = (acc / total).astype(BF16)
    m["l_bs"][...] = peak + jnp.log2(total)

    def combine(tag, groups):
        for group in groups:
            group.wait_recv()
        slots = "b" if tag == "bs" else "c"
        size = m["o_" + slots].shape[0]
        logs = [m["l_" + tag][...]] + [m["l_" + slots][n] for n in range(size)]
        peak = functools.reduce(jnp.maximum, logs)
        shares = [jnp.exp2(x - peak) for x in logs]
        total = functools.reduce(jnp.add, shares)
        acc = m["o_" + tag][...].astype(F32) * shares[0]
        for n in range(size):
            acc = acc + m["o_" + slots][n].astype(F32) * shares[n + 1]
        return acc / total, peak + jnp.log2(total)

    ob = [to_all(m["o_bs"], m["o_b"], group_n), to_all(m["l_bs"], m["l_b"], group_n)]

    mine = m["kv_full"].at[part_of(y * zn_n + zn, piece), part_of(c, FEATS)]
    m["kv_full"][part_of(y * zn_n + zn, piece), part_of(c, FEATS)] = gather(m["kv_cs"][...], kvc, m["kv_c"])
    kve = send_all([(mine, mine, dev) for dev in group_n], m["kv_b"])
    partners_next = [
        plan(m[name].at[pl.ds(8 - 8 * c, 2)], m[name].at[pl.ds(6 - 4 * c, 2)], partner)
        for name in ("kx", "vx")
    ]
    beside += partners_next
    inner = (z > 0) & (z < z_n - 1)

    def pass_on():
        for n, copy in enumerate(partners_next):
            for arriving in window[2 * n : 2 * n + 2]:
                arriving.wait_recv()
            copy.start()

    pl.when(inner)(pass_on)

    o, l = combine("bs", ob)
    m["o_cs"][...] = o.astype(BF16)
    m["l_cs"][...] = l
    oc = [to_all(m["o_cs"], m["o_c"], group_f), to_all(m["l_cs"], m["l_c"], group_f)]

    kve.wait_recv()
    mine = m["kv_full"].at[part_of(y, qc), part_of(c, FEATS)]
    kvd = send_all([(mine, mine, dev) for dev in group_j], m["kv_size"])
    pl.when(jnp.logical_not(inner))(pass_on)
    loads["rand"].wait()
    for copy in beside:
        copy.wait_recv()
    blocks = 2 * shards

    def queries_of(jb, pair):
        qb_here = m["q"][part_of(jb, BLOCK), :]
        return jnp.concatenate(
            [qb_here * head_mask(2 * pair, FEATS), qb_here * head_mask(2 * pair + 1, FEATS)],
            axis=0,
        )

    def attend_near(step, carry):
        jb = step // 2
        pair = step % 2
        q2 = queries_of(jb, pair)
        feats = part_of(pair, half)
        spots_x = [2 + jb + w for w in range(4)]
        spots_x += [
            jnp.clip(m["rand"][jb, n] - 2 * tm + 2 * SPREAD, 0, 9) for n in range(RAND)
        ]
        peak = None
        for n in range(7):
            s = dot_nt(m["kx"][spots_x[n]], q2) * LOG2_SCALE
            if n in (0, 1, 3):
                block = 2 * tm + jb + n - 2
                inside = (block >= 0) & (block < blocks)
                s = jnp.where(inside, s, NEG)
            m["s"][n] = s
            top = jnp.max(s, axis=0, keepdims=True)
            peak = top if peak is None else jnp.maximum(peak, top)
        total = jnp.zeros((1, 2 * BLOCK), F32)
        acc = jnp.zeros((half, 2 * BLOCK), F32)
        for at in ((0, 1), (2, 3), (4, 5), (6,)):
            weights, values = [], []
            for n in at:
                e = jnp.exp2(m["s"][n] - peak)
                total = total + jnp.sum(e, axis=0, keepdims=True)
                weights.append(e.astype(BF16))
                values.append(m["vx"][spots_x[n], feats, :])
            acc = acc + dot_nn(jnp.concatenate(values, axis=1), jnp.concatenate(weights, axis=0))
        m["peak"][step] = peak
        m["total"][step] = total
        m["acc"][step] = acc
        return carry

    for step in range(4):
        attend_near(step, 0)

    kvd.wait_recv()
    gv_t = m["kv_full"][:, FEATS:].astype(F32).T.astype(BF16)
    for b in range(2):
        m["gvt"][b] = gv_t[:, b * BLOCK : (b + 1) * BLOCK]

    def attend_global(step, carry):
        jb = step // 2
        pair = step % 2
        q2 = queries_of(jb, pair)
        feats = part_of(pair, half)
        s = dot_nt(m["kv_full"][:, :FEATS], q2) * LOG2_SCALE
        before = m["peak"][step]
        peak = jnp.maximum(before, jnp.max(s, axis=0, keepdims=True))
        e = jnp.exp2(s - peak)
        share = jnp.exp2(before - peak)
        total = m["total"][step] * share + jnp.sum(e, axis=0, keepdims=True)
        e = e.astype(BF16)
        acc = m["acc"][step] * share
        acc = acc + dot_nn(jnp.concatenate([m["gvt"][b, feats, :] for b in range(2)], axis=1), e)
        acc = acc / total
        for n in range(2):
            m["att_t"][part_of(pair * 2 + n, HEAD_DIM), part_of(jb, BLOCK)] = acc[
                n * HEAD_DIM : (n + 1) * HEAD_DIM, n * BLOCK : (n + 1) * BLOCK
            ]
        return carry

    for step in range(4):
        attend_global(step, 0)
    is_global = jnp.max(m["pick"][...].astype(F32), axis=1, keepdims=True)
    m["attl"][...] = jnp.where(is_global > 0.5, 0.0, m["att_t"][...].T)

    o, _ = combine("cs", oc)
    o_t = o.T
    o_t = jnp.concatenate([o_t[:qc], o_t[qc:]], axis=1).astype(BF16)
    m["o_full"][part_of(y, qc), part_of(c, half)] = o_t
    mine = m["o_full"].at[part_of(y, qc), part_of(c, half)]
    od = send_all([(mine, mine, dev) for dev in group_j], m["q_a"])
    od.wait_recv()

    placed = dot_nn(m["pick"][...], m["o_full"][...])
    m["att"][...] = (placed + m["attl"][...]).astype(BF16)
    per = TOK // heads
    x_steps = sorted(range(1, heads), key=lambda d: -min(d, heads - d))
    ax = {
        d: send(m["att"].at[part_of((hd + d) % heads, per)], m["asl"].at[d - 1], group_h[d - 1])
        for d in x_steps
    }
    mixed = dot_nn(m["att"][part_of(hd, per)], m["osl"][0])
    ow.wait_recv()
    for d in x_steps[::-1]:
        ax[d].wait_recv()
        mixed = mixed + dot_nn(m["asl"][d - 1], m["osl"][d])
    out_v[...] = mixed.astype(BF16)
    for copy in started:
        copy.wait_send()


def shards_fn(tokens, q_weight, k_weight, v_weight, o_weight, rand_blocks, global_pos):
    shards = lax.axis_size("tm")
    heads = lax.axis_size("head")
    split = split_of(shards)
    d = tokens.shape[1]
    scratch = scratch_of(split, heads, d)
    hbm = pl.BlockSpec(memory_space=pl.ANY)
    return pl.pallas_call(
        functools.partial(kernel, split, heads, list(scratch)),
        out_shape=jax.ShapeDtypeStruct((TOK // heads, d), BF16),
        in_specs=[hbm] * 7,
        out_specs=pl.BlockSpec(memory_space=pltpu.VMEM),
        scratch_shapes=list(scratch.values()),
        compiler_params=pltpu.CompilerParams(
            collective_id=0, has_side_effects=True, vmem_limit_bytes=VMEM_LIMIT
        ),
        name="layer",
    )(
        tokens,
        q_weight,
        k_weight,
        v_weight,
        o_weight,
        pltpu.with_memory_space_constraint(rand_blocks, pltpu.HBM),
        pltpu.with_memory_space_constraint(global_pos.reshape(1, GLOBALS), pltpu.HBM),
    )


def solution(mesh):
    placed = (
        P("tm", None),
        P(None, "head"),
        P(None, "head"),
        P(None, "head"),
        P("head", None),
        P("tm", None),
        P(),
    )
    return jax.shard_map(
        shards_fn, mesh=mesh, in_specs=placed, out_specs=P(("tm", "head"), None), check_vma=False
    )
```
